32 devices in a mesh: row: 8 (over y, x, core), col: 4 (over z).
Axes of the slice: x: 2, y: 2, z: 4, core: 2. Of those that a mesh axis runs over, the one named last changes fastest.
Arguments:
- skew_matrix: float32 [16384, 16384], P('row', 'col'), may hold values from -80 to 80, as said below
- first_reflector: float32 [16384, 128], P('row'), may hold values from -0.05625 to 0.05625
- first_factor: float32 [128, 128], replicated, may hold values from -0.6 to 1.5, as said below
- second_reflector: float32 [16384, 128], P('row'), may hold values from -0.05625 to 0.05625
- second_factor: float32 [128, 128], replicated, may hold values from -0.6 to 1.5, as said below
- vectors: float32 [16384, 4096], P('row', 'col'), may hold values from -6 to 6
Outputs:
- updated_matrix: float32 [16384, 16384], P('row', 'col')
- back_vectors: float32 [16384, 4096], P('row', 'col')
The draws below stay inside these ranges and needn't reach their ends.
Inputs may be any that keep to these rules, and one draw needn't show every extreme that they name: skew_matrix is skew-symmetric: entry (i, j) equals minus entry (j, i) exactly. first_factor is upper triangular with a positive diagonal. second_factor is upper triangular with a positive diagonal.
All inputs are finite; a program needn't handle non-finite values.
Results may differ from the reference program's by a relative error of at most 0.000059.
Values sent between devices are 32-bit elements; how exact they have to be, the bound alone decides.
A program may use at most 192 MiB of HBM per device.

```python
import jax
import jax.numpy as jnp
from jax import lax

N = 16384
NB = 128
K = 4096


def draw_skew_matrix(key, part):
    mkey = jax.random.fold_in(key, 3)
    base = jnp.clip(jax.random.normal(mkey, (N, N), jnp.float32), -6.0, 6.0)
    skew = (base - base.T) * 0.7071
    return skew


def factor_draw(key):
    diagonal = jax.random.uniform(jax.random.fold_in(key, 1), (NB,), jnp.float32, 0.5, 1.5)
    upper = jnp.clip(0.1 * jax.random.normal(jax.random.fold_in(key, 2), (NB, NB), jnp.float32), -0.6, 0.6)
    return jnp.triu(upper, 1) + jnp.diag(diagonal)


def draw_first_factor(key, part):
    return factor_draw(jax.random.fold_in(key, 11))


def draw_second_factor(key, part):
    return factor_draw(jax.random.fold_in(key, 12))


def level_of(stream_key, extent, cuts, smallest, high):
    loudness = 1.0
    for position, blocks in cuts:
        heights = jax.random.uniform(jax.random.fold_in(jax.random.fold_in(stream_key, 6), position), (blocks,), jnp.float32, smallest / len(cuts), high / len(cuts))
        loudness = loudness * jnp.repeat(jnp.exp(heights), extent[position] // blocks).reshape((-1,) + (1,) * (len(extent) - 1 - position))
    return loudness


def centred(stream_key, shape, scale, limit, cuts=(), held_as=jnp.bfloat16):
    entries = jax.random.normal(stream_key, shape, jnp.float32) * scale
    if len(cuts) > 0:
        entries = level_of(stream_key, shape, cuts, -0.22, 0.18) * entries
    return jnp.clip(entries, min=-limit, max=limit).astype(held_as)


def setup_inputs(seed: int = 0) -> dict:
    keys = jax.random.split(jax.random.key(seed), 7)
    return {
        "skew_matrix": draw_skew_matrix(jax.random.fold_in(keys[6], 71), 0),
        "first_reflector": centred(keys[1], (N, NB), (1.2 / N**0.5), 0.05625, ((0, 8),), jnp.float32),
        "first_factor": draw_first_factor(jax.random.fold_in(keys[6], 71), 0),
        "second_reflector": centred(keys[3], (N, NB), (1.2 / N**0.5), 0.05625, ((0, 8),), jnp.float32),
        "second_factor": draw_second_factor(jax.random.fold_in(keys[6], 71), 0),
        "vectors": centred(keys[5], (N, K), 1.0, 6.0, ((0, 8), (1, 4)), jnp.float32),
    }


def multiply(left, right):
    return jnp.dot(left, right, precision=lax.Precision.HIGHEST, preferred_element_type=jnp.float32)


def transform(matrix, reflector, factor):
    product = multiply(matrix, reflector)
    wide = multiply(product, factor)
    gram = multiply(reflector.T, product)
    correction = multiply(multiply(factor.T, gram), factor)
    fixed = wide - 0.5 * multiply(reflector, correction)
    left = jnp.concatenate([reflector, -fixed], axis=1)
    right = jnp.concatenate([fixed, reflector], axis=1)
    return matrix + multiply(left, right.T)


def back_apply(vectors, reflector, factor):
    sums = multiply(reflector.T, vectors)
    return vectors - multiply(reflector, multiply(factor, sums))


def reference(skew_matrix, first_reflector, first_factor, second_reflector, second_factor, vectors):
    inner = transform(skew_matrix, first_reflector, first_factor)
    updated_matrix = transform(inner, second_reflector, second_factor)
    middle = back_apply(vectors, second_reflector, second_factor)
    back_vectors = back_apply(middle, first_reflector, first_factor)
    return updated_matrix, back_vectors
```

```python
import functools

import jax
import jax.numpy as jnp
from jax import lax
from jax.experimental import pallas as pl
from jax.experimental.pallas import tpu as pltpu
from jax.sharding import PartitionSpec as P

MESH = pl.DeviceIdType.MESH
F32, BF16 = jnp.float32, jnp.bfloat16
NN = ((1,), (0,))
TN = ((0,), (0,))
NT = ((1,), (1,))
VMEM_BYTES = 61 * 2**20


def dot(left, right, dims=NN):
    return lax.dot_general(left, right, (dims, ((), ())), preferred_element_type=F32)


def exact(left, right, dims=NN):
    return lax.dot_general(
        left, right, (dims, ((), ())), precision=lax.Precision.HIGHEST, preferred_element_type=F32
    )


def split(value):
    high = value.astype(BF16)
    return high, (value - high.astype(F32)).astype(BF16)


def dot3(left, right, dims=NN):
    lh, ll = split(left)
    rh, rl = split(right)
    return dot(lh, rh, dims) + dot(ll, rh, dims) + dot(lh, rl, dims)


def pick(index, table):
    return sum(jnp.where(index == i, v, 0) for i, v in enumerate(table))


def aligned(start, size):
    return pl.ds(pl.multiple_of(start, size), size)


class Plan:
    def __init__(self, rows, cols, n, nc, kc, nb):
        self.rows, self.cols, self.n, self.nc, self.kc, self.nb = rows, cols, n, nc, kc, nb
        self.nb2 = 2 * nb
        self.w = min(512, kc, nc // 2)
        self.nm, self.nv = nc // self.w, kc // self.w
        self.nch = self.nm + self.nv
        self.bits = (rows // 2).bit_length() - 1
        self.stages = 1 + self.bits
        self.nz = self.nm // 2
        self.nsub = 4
        self.np = 8
        self.gram_tick = max(self.nm + self.stages, self.np + cols - 1)
        self.done = 2 * self.stages
        self.ticks = max(self.nm + self.done + 1, self.nch + self.done, self.gram_tick + 3)
        self.piece = nb // rows


def kernel(
    p,
    m_hbm, vec_hbm, v1_hbm, v2_hbm, f1, f2,
    t_hbm, lp_hbm, vc_hbm, y_hbm, vj_hbm,
    vown, vt, lq, mbuf, tbuf, pt, pg, recvs, pr, vc, lp, yb,
    cx, cr, cf, gm, gr, gf, comp, skw,
    rs_s, rs_r, ag_s, ag_r, zu_s, zd_s, z_r, va_s, va_r, vb_s, vb_r, vx_s, vx_r,
    c1_s, c1_r, c2_s, c2_r, g1_s, g1_r, g2_s, g2_r, m_in, t_in, t_out, io,
):
    r, c = lax.axis_index("row"), lax.axis_index("col")
    rows, cols, w, S = p.rows, p.cols, p.w, p.stages
    core = r % 2
    q = r // 2

    def remote(src, dst, ssem, rsem, row, col):
        return pltpu.make_async_remote_copy(
            src_ref=src, dst_ref=dst, send_sem=ssem, recv_sem=rsem, device_id=(row, col), device_id_type=MESH
        )

    barrier = pltpu.get_barrier_semaphore()
    for d in range(1, rows):
        pl.semaphore_signal(barrier, inc=1, device_id=((r + d) % rows, c), device_id_type=MESH)
    for d in range(1, cols):
        pl.semaphore_signal(barrier, inc=1, device_id=(r, (c + d) % cols), device_id_type=MESH)

    def flip(bit):
        return r + bit * (1 - 2 * ((r // bit) % 2)), (r // bit) % 2

    partner, mine = [], []
    for s in range(S):
        if s == 0:
            who, bit = flip(1)
        else:
            a, abit = flip(1 << s)
            b, bbit = flip(1 << (s % p.bits + 1))
            who, bit = a + core * (b - a), abit + core * (bbit - abit)
        partner.append(who)
        mine.append(bit)
    size = [p.nb2 >> s for s in range(S + 1)]
    off = [0]
    for s in range(S):
        off.append(off[s] + mine[s] * size[s + 1])

    def rows_of(s):
        return aligned(off[s], size[s]) if s else pl.ds(0, size[0])

    def other_rows(s):
        return aligned(off[s] + (1 - mine[s]) * size[s + 1], size[s + 1])

    gray = [i ^ (i >> 1) for i in range(cols)]
    back = [gray.index(i) for i in range(cols)]
    place = pick(q, back)
    pos = (place - pick(c, back) + cols) % cols
    nxt = 2 * pick((place + 1) % cols, gray) + core
    prv = 2 * pick((place + cols - 1) % cols, gray) + core
    posb = (cols - pos) % cols

    def column(j):
        return pl.multiple_of((j % 2) * (p.nc // 2) + (j // 2) * w, w)

    def m_copy(j, buf, slot, sem):
        return pltpu.make_async_copy(m_hbm.at[:, pl.ds(column(j), w)], buf.at[slot], sem)

    def v_copy(j, slot):
        return pltpu.make_async_copy(
            vec_hbm.at[:, aligned((j - p.nm) * w, w)], mbuf.at[slot], m_in.at[slot]
        )

    def fetch(j):
        @pl.when(j < p.nm)
        def _():
            m_copy(j, mbuf, j % 2, m_in.at[j % 2]).start()

        @pl.when(jnp.logical_and(j >= p.nm, j < p.nch))
        def _():
            v_copy(j, j % 2).start()

    own1 = pltpu.make_async_copy(v1_hbm, vown.at[:, pl.ds(0, p.nb)], io.at[0])
    own2 = pltpu.make_async_copy(v2_hbm, vown.at[:, pl.ds(p.nb, p.nb)], io.at[1])
    own1.start()
    own2.start()
    m_copy(0, mbuf, 0, m_in.at[0]).start()
    own1.wait()
    own2.wait()
    vj_out = pltpu.make_async_copy(vown, vj_hbm, io.at[2])
    vj_out.start()
    step = 256
    nblk = p.n // step

    def prepare(i, _):
        at = aligned(i * step, step)
        high, low = split(vown[at, :].T)
        vt[pl.ds(0, p.nb2), at] = high
        vt[pl.ds(p.nb2, p.nb2), at] = low
        return 0

    lax.fori_loop(0, nblk, prepare, 0)

    @pl.when(pos == 0)
    def _():
        vc[core] = vown[...]

    def cross_part(i, total):
        at = aligned(i * step, step)
        x2h, x2l = split(vown[at, pl.ds(p.nb, p.nb)])
        th, tl = vt[pl.ds(0, p.nb), at], vt[pl.ds(p.nb2, p.nb), at]
        return total + (dot(th, x2h) + dot(tl, x2h) + dot(th, x2l))

    cx[...] = lax.fori_loop(0, nblk, cross_part, jnp.zeros((p.nb, p.nb), F32))

    pl.semaphore_wait(barrier, rows - 1 + cols - 1)

    pc = p.piece

    def cross_sum(d):
        to = (r + d) % rows
        return remote(cx.at[aligned(to * pc, pc)], cr.at[d], c1_s.at[d], c1_r.at[d], to, c)

    def cross_all(d):
        to = (r + d) % rows
        at = aligned(r * pc, pc)
        return remote(cf.at[at], cf.at[at], c2_s.at[d], c2_r.at[d], to, c)

    def cross_got(d):
        frm = (r + rows - d) % rows
        at = aligned(frm * pc, pc)
        return remote(cf.at[at], cf.at[at], c2_s.at[d], c2_r.at[d], frm, c)

    for d in range(1, rows):
        cross_sum(d).start()

    def rs(j, s):
        return remote(pt.at[j, other_rows(s)], recvs[s].at[j], rs_s.at[j, s], rs_r.at[j, s], partner[s], c)

    def ag(j, a):
        s = S - 1 - a
        at = rows_of(s + 1)
        return remote(pg.at[j, at], pg.at[j, at], ag_s.at[j, a], ag_r.at[j, a], partner[s], c)

    def ag_got(j, a):
        s = S - 1 - a
        at = other_rows(s)
        return remote(pg.at[j, at], pg.at[j, at], ag_s.at[j, a], ag_r.at[j, a], partner[s], c)

    sub = p.nb2 // p.nsub

    def zcopy(src, i, s, sems, to):
        at = aligned(s * sub, sub)
        return remote(src.at[at], pr.at[i, at], sems.at[i, s], z_r.at[i, s], r, to)

    half = p.n // 2
    vpc = half // p.np

    def ring(i, base, ssem, rsem, to):
        at = aligned(base + i * vpc, vpc)
        return remote(vc.at[core, at], vc.at[core, at], ssem.at[i], rsem.at[i], to, c)

    def cross_core(which, i, base, b):
        at = aligned(base + i * vpc, vpc)
        return remote(vc.at[which, at], vc.at[which, at], vx_s.at[b, i], vx_r.at[b, i], partner[0], c)

    def gram_sum(d):
        to = (c + d) % cols
        return remote(gm, gr.at[d], g1_s.at[d], g1_r.at[d], r, to)

    def gram_all(d):
        at = rows_of(S)
        return remote(gf.at[at], gf.at[at], g2_s.at[d], g2_r.at[d], (r + d) % rows, c)

    def gram_wait(d):
        at = rows_of(S)
        return remote(gf.at[at], gf.at[at], g2_s.at[d], g2_r.at[d], (r + d) % rows, c)

    def tick(t, _):
        for a in range(S - 1, -1, -1):
            j = t - S - 1 - a

            @pl.when(jnp.logical_and(j >= 0, j < p.nch))
            def _():
                ag_got(j, a).wait_recv()
                if a < S - 1:
                    ag(j, a + 1).start()

        j = t - p.done

        @pl.when(jnp.logical_and(jnp.logical_and(j >= 0, j < p.nm), jnp.logical_and(j % 2 == core, c == q)))
        def _():
            i = j // 2
            for s in range(p.nsub):
                @pl.when(c < cols - 1)
                def _():
                    zcopy(pg.at[j], i, s, zu_s, c + 1).start()

                @pl.when(c > 0)
                def _():
                    zcopy(pg.at[j], i, s, zd_s, c - 1).start()
            pr[i] = pg[j]

        for s in range(S - 1, -1, -1):
            j = t - 1 - s

            @pl.when(jnp.logical_and(j >= 0, j < p.nch))
            def _():
                rs(j, s).wait_recv()
                at = rows_of(s + 1)
                if s < S - 1:
                    pt[j, at] = pt[j, at] + recvs[s][j]
                    rs(j, s + 1).start()
                else:
                    pg[j, at] = pt[j, at] + recvs[s][j]
                    ag(j, 0).start()

        ia = t - pos

        @pl.when(jnp.logical_and(ia >= 0, ia < p.np))
        def _():
            @pl.when(pos > 0)
            def _():
                ring(ia, 0, va_s, va_r, prv).wait_recv()

            @pl.when(pos < cols - 1)
            def _():
                ring(ia, 0, va_s, va_r, nxt).start()

            cross_core(core, ia, 0, 0).start()

        ib = t - posb

        @pl.when(jnp.logical_and(ib >= 0, ib < p.np))
        def _():
            @pl.when(posb > 0)
            def _():
                ring(ib, half, vb_s, vb_r, nxt).wait_recv()

            @pl.when(posb < cols - 1)
            def _():
                ring(ib, half, vb_s, vb_r, prv).start()

            cross_core(core, ib, half, 1).start()

        @pl.when(t == 2)
        def _():
            at = aligned(r * pc, pc)
            total = cx[at]
            for d in range(1, rows):
                cross_sum(d).wait_recv()
                total = total + cr[d]
            cf[at] = total
            for d in range(1, rows):
                cross_all(d).start()

        @pl.when(t == p.gram_tick)
        def _():
            for b in range(2):
                for i in range(p.np):
                    cross_core(1 - core, i, b * half, b).wait_recv()
            pltpu.make_async_copy(vc, vc_hbm, io.at[3]).start()
            at = rows_of(S)

            def part(j, total):
                n0 = aligned((j // 2) * w, w)
                return total + dot3(pg[j, at], vc[j % 2, n0, :])

            gm[...] = lax.fori_loop(0, p.nm, part, jnp.zeros((size[S], p.nb2), F32))
            for d in range(1, cols):
                gram_sum(d).start()

        @pl.when(t == p.gram_tick + 1)
        def _():
            total = gm[...]
            for d in range(1, cols):
                gram_sum(d).wait_recv()
                total = total + gr[d]
            gf[rows_of(S)] = total
            for d in range(1, rows):
                gram_all(d).start()

        @pl.when(t == p.gram_tick + 2)
        def _():
            for d in range(1, rows):
                gram_wait(d).wait_recv()
            nb = p.nb
            one, two = f1[...], f2[...]
            cross = cf[...]
            g11, g21, g22 = gf[:nb, :nb], gf[nb:, :nb], gf[nb:, nb:]
            x1 = exact(exact(one, g11, TN), one)
            key = exact(one, g21, ((0,), (1,))) - 0.5 * exact(x1, cross, TN)
            twist = exact(cross, key, TN)
            gram2 = g22 + twist - twist.T
            x2 = exact(exact(two, gram2, TN), two)
            mixed = exact(key + 0.5 * exact(x1, cross), two)
            skw[:nb, :nb] = 0.5 * (x1.T - x1)
            skw[:nb, nb:] = mixed
            skw[nb:, :nb] = -mixed.T
            skw[nb:, nb:] = 0.5 * (x2.T - x2)

        @pl.when(t + 1 < p.nch)
        def _():
            fetch(t + 1)

        @pl.when(t < p.nch)
        def _():
            slot = t % 2
            pltpu.make_async_copy(mbuf.at[slot], mbuf.at[slot], m_in.at[slot]).wait()
            high, low = split(mbuf[slot])
            both = dot(vt[...], high)
            pt[t] = both[: p.nb2] + both[p.nb2 :] + dot(vt[pl.ds(0, p.nb2)], low)
            rs(t, 0).start()

        jn = t + 1 - p.done

        @pl.when(jnp.logical_and(jn >= 0, jn < p.nm))
        def _():
            @pl.when(jn >= 3)
            def _():
                pltpu.make_async_copy(
                    tbuf.at[jn % 3], t_hbm.at[:, pl.ds(column(jn), w)], t_out.at[jn % 3]
                ).wait()

            m_copy(jn, tbuf, jn % 3, t_in.at[jn % 3]).start()

        @pl.when(t == p.done - 1)
        def _():
            for d in range(1, rows):
                cross_got(d).wait_recv()
            nb = p.nb
            comp[:nb, :nb] = f1[...]
            comp[:nb, nb:] = -exact(exact(f1[...], cf[...]), f2[...])
            comp[nb:, :nb] = jnp.zeros((nb, nb), F32)
            comp[nb:, nb:] = f2[...]

            def build(i, _):
                at = aligned(i * step, step)
                high, low = split(dot3(vown[at, :], comp[...], NT))
                lq[0, at] = high
                lq[1, at] = low
                return 0

            lax.fori_loop(0, nblk, build, 0)

        j = t - p.done

        @pl.when(jnp.logical_and(j >= 0, j < p.nm))
        def _():
            slot = j % 3
            m_copy(j, tbuf, slot, t_in.at[slot]).wait()
            high, low = split(pg[j])

            def add(i, _):
                at = aligned(i * step, step)
                lh = lq[0, at]
                tbuf[slot, at] = tbuf[slot, at] - (dot(lh, high) + dot(lq[1, at], high) + dot(lh, low))
                return 0

            lax.fori_loop(0, nblk, add, 0)
            pltpu.make_async_copy(tbuf.at[slot], t_hbm.at[:, pl.ds(column(j), w)], t_out.at[slot]).start()

        @pl.when(jnp.logical_and(j >= p.nm, j < p.nch))
        def _():
            yb[j - p.nm] = dot3(comp[...], pg[j])

        j = t - p.done - 1

        @pl.when(jnp.logical_and(jnp.logical_and(j >= 0, j < p.nm), jnp.logical_and(j % 2 == core, c != q)))
        def _():
            i = j // 2
            for s in range(p.nsub):
                zcopy(pr.at[i], i, s, zu_s, c).wait_recv()

                @pl.when(jnp.logical_and(c > q, c < cols - 1))
                def _():
                    zcopy(pr.at[i], i, s, zu_s, c + 1).start()

                @pl.when(jnp.logical_and(c < q, c > 0))
                def _():
                    zcopy(pr.at[i], i, s, zd_s, c - 1).start()

        return 0

    lax.fori_loop(0, p.ticks, tick, 0)

    def left(i, _):
        for b in range(w // step):
            at = aligned(i * w + b * step, step)
            mixed = dot3(pr[i, :, pl.ds(b * step, step)].T, comp[...])
            lp[at] = dot3(vown[at, :], skw[...]) - mixed
        return 0

    lax.fori_loop(0, p.nz, left, 0)
    lp_out = pltpu.make_async_copy(lp, lp_hbm, io.at[0])
    lp_out.start()
    outs = []
    for b in range(p.nv):
        copy = pltpu.make_async_copy(yb.at[b], y_hbm.at[:, pl.ds(b * w, w)], io.at[4 + b])
        copy.start()
        outs.append(copy)

    def drain(j, _):
        for s in range(S):
            rs(j, s).wait_send()
            ag(j, s).wait_send()
        return 0

    lax.fori_loop(0, p.nch, drain, 0)

    def drain_z(i, _):
        for s in range(p.nsub):
            @pl.when(jnp.logical_and(c >= q, c < cols - 1))
            def _():
                zcopy(pr.at[i], i, s, zu_s, c + 1).wait_send()

            @pl.when(jnp.logical_and(c <= q, c > 0))
            def _():
                zcopy(pr.at[i], i, s, zd_s, c - 1).wait_send()
        return 0

    lax.fori_loop(0, p.nz, drain_z, 0)

    def drain_v(i, _):
        @pl.when(pos < cols - 1)
        def _():
            ring(i, 0, va_s, va_r, nxt).wait_send()

        @pl.when(posb < cols - 1)
        def _():
            ring(i, half, vb_s, vb_r, prv).wait_send()

        cross_core(core, i, 0, 0).wait_send()
        cross_core(core, i, half, 1).wait_send()
        return 0

    lax.fori_loop(0, p.np, drain_v, 0)
    for d in range(1, rows):
        cross_sum(d).wait_send()
        cross_all(d).wait_send()
        gram_all(d).wait_send()
    for d in range(1, cols):
        gram_sum(d).wait_send()
    for j in range(max(0, p.nm - 3), p.nm):
        pltpu.make_async_copy(tbuf.at[j % 3], t_hbm.at[:, pl.ds(column(j), w)], t_out.at[j % 3]).wait()
    pltpu.make_async_copy(vc, vc_hbm, io.at[3]).wait()
    vj_out.wait()
    lp_out.wait()
    for copy in outs:
        copy.wait()


def exchange(p, matrix, vectors, first, second, factor1, factor2):
    n, nb2, w, S = p.n, p.nb2, p.w, p.stages
    hbm = pl.BlockSpec(memory_space=pl.ANY)
    vmem = pl.BlockSpec(memory_space=pltpu.VMEM)
    dma = pltpu.SemaphoreType.DMA

    def body(*refs):
        ins, rest = refs[:11], refs[11:]
        before, rest = rest[:7], rest[7:]
        recvs, rest = rest[:S], rest[S:]
        kernel(p, *ins, *before, recvs, *rest)

    shape = lambda *s: jax.ShapeDtypeStruct(s, F32)
    scratch = [
        pltpu.VMEM((n, nb2), F32),
        pltpu.VMEM((2 * nb2, n), BF16),
        pltpu.VMEM((2, n, nb2), BF16),
        pltpu.VMEM((2, n, w), F32),
        pltpu.VMEM((3, n, w), F32),
        pltpu.VMEM((p.nch, nb2, w), F32),
        pltpu.VMEM((p.nch, nb2, w), F32),
    ]
    scratch += [pltpu.VMEM((p.nch, nb2 >> (s + 1), w), F32) for s in range(S)]
    scratch += [
        pltpu.VMEM((p.nz, nb2, w), F32),
        pltpu.VMEM((2, n, nb2), F32),
        pltpu.VMEM((n, nb2), F32),
        pltpu.VMEM((p.nv, nb2, w), F32),
        pltpu.VMEM((p.nb, p.nb), F32),
        pltpu.VMEM((p.rows, p.piece, p.nb), F32),
        pltpu.VMEM((p.nb, p.nb), F32),
        pltpu.VMEM((nb2 >> S, nb2), F32),
        pltpu.VMEM((p.cols, nb2 >> S, nb2), F32),
        pltpu.VMEM((nb2, nb2), F32),
        pltpu.VMEM((nb2, nb2), F32),
        pltpu.VMEM((nb2, nb2), F32),
    ]
    scratch += [dma((p.nch, S)) for _ in range(4)]
    scratch += [dma((p.nz, p.nsub)) for _ in range(3)]
    scratch += [dma((p.np,)) for _ in range(4)] + [dma((2, p.np)) for _ in range(2)]
    scratch += [dma((p.rows,)) for _ in range(4)]
    scratch += [dma((p.cols,)) for _ in range(2)] + [dma((p.rows,)) for _ in range(2)]
    scratch += [dma((2,)), dma((3,)), dma((3,)), dma((4 + p.nv,))]
    return pl.pallas_call(
        body,
        out_shape=[shape(n, p.nc), shape(n, nb2), shape(2, n, nb2), shape(nb2, p.kc), shape(n, nb2)],
        in_specs=[hbm] * 4 + [vmem] * 2,
        out_specs=[hbm] * 5,
        scratch_shapes=scratch,
        compiler_params=pltpu.CompilerParams(
            collective_id=0, has_side_effects=True, vmem_limit_bytes=VMEM_BYTES
        ),
        cost_estimate=pl.CostEstimate(
            flops=12 * n * p.nc * nb2, bytes_accessed=12 * n * p.nc, transcendentals=0
        ),
    )(matrix, vectors, first, second, factor1, factor2)


def solution(mesh):
    rows, cols = mesh.shape["row"], mesh.shape["col"]

    def shards(matrix, first, factor1, second, factor2, vectors):
        p = Plan(rows, cols, *matrix.shape, vectors.shape[1], first.shape[1])
        partly, left, panel, inner, joined = exchange(p, matrix, vectors, first, second, factor1, factor2)
        high = functools.partial(
            lax.dot_general, precision=lax.Precision.HIGH, preferred_element_type=F32
        )
        back = vectors - high(joined, inner, (NN, ((), ())))
        panel = panel.reshape(2 * p.n, 2 * p.nb)
        return partly - high(left, panel, (NT, ((), ()))), back

    in_specs = (P("row", "col"), P("row", None), P(), P("row", None), P(), P("row", "col"))
    out_specs = (P("row", "col"), P("row", "col"))
    return jax.shard_map(shards, mesh=mesh, in_specs=in_specs, out_specs=out_specs, check_vma=False)
```

```python
import functools

import jax
import jax.numpy as jnp
from jax import lax
from jax.experimental import pallas as pl
from jax.experimental.pallas import tpu as pltpu
from jax.sharding import PartitionSpec as P

MESH = pl.DeviceIdType.MESH
F32, BF16 = jnp.float32, jnp.bfloat16
NN = ((1,), (0,))
TN = ((0,), (0,))
NT = ((1,), (1,))
VMEM_BYTES = 61 * 2**20


def dot(left, right, dims=NN):
    return lax.dot_general(left, right, (dims, ((), ())), preferred_element_type=F32)


def exact(left, right, dims=NN):
    return lax.dot_general(
        left, right, (dims, ((), ())), precision=lax.Precision.HIGHEST, preferred_element_type=F32
    )


def split(value):
    high = value.astype(BF16)
    return high, (value - high.astype(F32)).astype(BF16)


def dot3(left, right, dims=NN):
    lh, ll = split(left)
    rh, rl = split(right)
    return dot(lh, rh, dims) + dot(ll, rh, dims) + dot(lh, rl, dims)


def pick(index, table):
    return sum(jnp.where(index == i, v, 0) for i, v in enumerate(table))


def aligned(start, size):
    return pl.ds(pl.multiple_of(start, size), size)


class Plan:
    def __init__(self, rows, cols, n, nc, kc, nb):
        self.rows, self.cols, self.n, self.nc, self.kc, self.nb = rows, cols, n, nc, kc, nb
        self.nb2 = 2 * nb
        self.w = min(512, kc, nc // 2)
        self.nm, self.nv = nc // self.w, kc // self.w
        self.nch = self.nm + self.nv
        self.bits = (rows // 2).bit_length() - 1
        self.stages = 1 + self.bits
        self.nz = self.nm // 2
        self.nsub = 4
        self.np = 8
        self.lag, self.zlag, self.vlag = 1, 1, 1
        self.gram_tick = max(self.nm + self.lag * self.stages, self.np + self.vlag * cols)
        self.done = self.lag * 2 * self.stages
        self.ticks = max(
            self.nm + self.done + self.zlag * (cols - 1),
            self.nch + self.done,
            self.gram_tick + 2 * self.lag + 1,
        )
        self.piece = nb // rows


def kernel(
    p,
    m_hbm, vec_hbm, v1_hbm, v2_hbm, f1, f2,
    t_hbm, lp_hbm, vc_hbm, y_hbm, vj_hbm,
    vown, vt, lq, mbuf, tbuf, pt, pg, recvs, pr, vc, lp, yb,
    cx, cr, cf, gm, gr, gf, comp, skw,
    rs_s, rs_r, ag_s, ag_r, zu_s, zd_s, z_r, va_s, va_r, vb_s, vb_r, vx_s, vx_r,
    c1_s, c1_r, c2_s, c2_r, g1_s, g1_r, g2_s, g2_r, m_in, t_in, t_out, io,
):
    r, c = lax.axis_index("row"), lax.axis_index("col")
    rows, cols, w, S = p.rows, p.cols, p.w, p.stages
    core = r % 2
    q = r // 2

    def remote(src, dst, ssem, rsem, row, col):
        return pltpu.make_async_remote_copy(
            src_ref=src, dst_ref=dst, send_sem=ssem, recv_sem=rsem, device_id=(row, col), device_id_type=MESH
        )

    barrier = pltpu.get_barrier_semaphore()
    for d in range(1, rows):
        pl.semaphore_signal(barrier, inc=1, device_id=((r + d) % rows, c), device_id_type=MESH)
    for d in range(1, cols):
        pl.semaphore_signal(barrier, inc=1, device_id=(r, (c + d) % cols), device_id_type=MESH)

    def flip(bit):
        return r + bit * (1 - 2 * ((r // bit) % 2)), (r // bit) % 2

    partner, mine = [], []
    for s in range(S):
        if s == 0:
            who, bit = flip(1)
        else:
            a, abit = flip(1 << s)
            b, bbit = flip(1 << (s % p.bits + 1))
            who, bit = a + core * (b - a), abit + core * (bbit - abit)
        partner.append(who)
        mine.append(bit)
    size = [p.nb2 >> s for s in range(S + 1)]
    off = [0]
    for s in range(S):
        off.append(off[s] + mine[s] * size[s + 1])

    def rows_of(s):
        return aligned(off[s], size[s]) if s else pl.ds(0, size[0])

    def other_rows(s):
        return aligned(off[s] + (1 - mine[s]) * size[s + 1], size[s + 1])

    gray = [i ^ (i >> 1) for i in range(cols)]
    back = [gray.index(i) for i in range(cols)]
    place = pick(q, back)
    pos = (place - pick(c, back) + cols) % cols
    nxt = 2 * pick((place + 1) % cols, gray) + core
    prv = 2 * pick((place + cols - 1) % cols, gray) + core
    posb = (cols - pos) % cols
    hops = jnp.where(c > q, c - q, q - c)

    def column(j):
        return pl.multiple_of((j % 2) * (p.nc // 2) + (j // 2) * w, w)

    def m_copy(j, buf, slot, sem):
        return pltpu.make_async_copy(m_hbm.at[:, pl.ds(column(j), w)], buf.at[slot], sem)

    def v_copy(j, slot):
        return pltpu.make_async_copy(
            vec_hbm.at[:, aligned((j - p.nm) * w, w)], mbuf.at[slot], m_in.at[slot]
        )

    def fetch(j):
        @pl.when(j < p.nm)
        def _():
            m_copy(j, mbuf, j % 2, m_in.at[j % 2]).start()

        @pl.when(jnp.logical_and(j >= p.nm, j < p.nch))
        def _():
            v_copy(j, j % 2).start()

    own1 = pltpu.make_async_copy(v1_hbm, vown.at[:, pl.ds(0, p.nb)], io.at[0])
    own2 = pltpu.make_async_copy(v2_hbm, vown.at[:, pl.ds(p.nb, p.nb)], io.at[1])
    own1.start()
    own2.start()
    m_copy(0, mbuf, 0, m_in.at[0]).start()
    own1.wait()
    own2.wait()
    vj_out = pltpu.make_async_copy(vown, vj_hbm, io.at[2])
    vj_out.start()
    step = 256
    nblk = p.n // step

    def prepare(i, _):
        at = aligned(i * step, step)
        high, low = split(vown[at, :].T)
        vt[pl.ds(0, p.nb2), at] = high
        vt[pl.ds(p.nb2, p.nb2), at] = low
        return 0

    lax.fori_loop(0, nblk, prepare, 0)

    @pl.when(pos == 0)
    def _():
        vc[core] = vown[...]

    def cross_part(i, total):
        at = aligned(i * step, step)
        x2h, x2l = split(vown[at, pl.ds(p.nb, p.nb)])
        th, tl = vt[pl.ds(0, p.nb), at], vt[pl.ds(p.nb2, p.nb), at]
        return total + (dot(th, x2h) + dot(tl, x2h) + dot(th, x2l))

    cx[...] = lax.fori_loop(0, nblk, cross_part, jnp.zeros((p.nb, p.nb), F32))

    pl.semaphore_wait(barrier, rows - 1 + cols - 1)

    pc = p.piece

    def cross_sum(d):
        to = (r + d) % rows
        return remote(cx.at[aligned(to * pc, pc)], cr.at[d], c1_s.at[d], c1_r.at[d], to, c)

    def cross_all(d):
        to = (r + d) % rows
        at = aligned(r * pc, pc)
        return remote(cf.at[at], cf.at[at], c2_s.at[d], c2_r.at[d], to, c)

    def cross_got(d):
        frm = (r + rows - d) % rows
        at = aligned(frm * pc, pc)
        return remote(cf.at[at], cf.at[at], c2_s.at[d], c2_r.at[d], frm, c)

    for d in range(1, rows):
        cross_sum(d).start()

    def rs(j, s):
        return remote(pt.at[j, other_rows(s)], recvs[s].at[j], rs_s.at[j, s], rs_r.at[j, s], partner[s], c)

    def ag(j, a):
        s = S - 1 - a
        at = rows_of(s + 1)
        return remote(pg.at[j, at], pg.at[j, at], ag_s.at[j, a], ag_r.at[j, a], partner[s], c)

    def ag_got(j, a):
        s = S - 1 - a
        at = other_rows(s)
        return remote(pg.at[j, at], pg.at[j, at], ag_s.at[j, a], ag_r.at[j, a], partner[s], c)

    sub = p.nb2 // p.nsub

    def zcopy(src, i, s, sems, to):
        at = aligned(s * sub, sub)
        return remote(src.at[at], pr.at[i, at], sems.at[i, s], z_r.at[i, s], r, to)

    half = p.n // 2
    vpc = half // p.np

    def ring(i, base, ssem, rsem, to):
        at = aligned(base + i * vpc, vpc)
        return remote(vc.at[core, at], vc.at[core, at], ssem.at[i], rsem.at[i], to, c)

    def cross_core(which, i, base, b):
        at = aligned(base + i * vpc, vpc)
        return remote(vc.at[which, at], vc.at[which, at], vx_s.at[b, i], vx_r.at[b, i], partner[0], c)

    def gram_sum(d):
        to = (c + d) % cols
        return remote(gm, gr.at[d], g1_s.at[d], g1_r.at[d], r, to)

    def gram_all(d):
        at = rows_of(S)
        return remote(gf.at[at], gf.at[at], g2_s.at[d], g2_r.at[d], (r + d) % rows, c)

    def gram_wait(d):
        at = rows_of(S)
        return remote(gf.at[at], gf.at[at], g2_s.at[d], g2_r.at[d], (r + d) % rows, c)

    def tick(t, _):
        for a in range(S - 1, -1, -1):
            j = t - p.lag * (S + 1 + a)

            @pl.when(jnp.logical_and(j >= 0, j < p.nch))
            def _():
                ag_got(j, a).wait_recv()
                if a < S - 1:
                    ag(j, a + 1).start()

        j = t - p.done

        @pl.when(jnp.logical_and(jnp.logical_and(j >= 0, j < p.nm), jnp.logical_and(j % 2 == core, c == q)))
        def _():
            i = j // 2
            for s in range(p.nsub):
                @pl.when(c < cols - 1)
                def _():
                    zcopy(pg.at[j], i, s, zu_s, c + 1).start()

                @pl.when(c > 0)
                def _():
                    zcopy(pg.at[j], i, s, zd_s, c - 1).start()
            pr[i] = pg[j]

        j = t - p.done - p.zlag * hops

        @pl.when(jnp.logical_and(jnp.logical_and(j >= 0, j < p.nm), jnp.logical_and(j % 2 == core, c != q)))
        def _():
            i = j // 2
            for s in range(p.nsub):
                zcopy(pr.at[i], i, s, zu_s, c).wait_recv()

                @pl.when(jnp.logical_and(c > q, c < cols - 1))
                def _():
                    zcopy(pr.at[i], i, s, zu_s, c + 1).start()

                @pl.when(jnp.logical_and(c < q, c > 0))
                def _():
                    zcopy(pr.at[i], i, s, zd_s, c - 1).start()

        for s in range(S - 1, -1, -1):
            j = t - p.lag * (1 + s)

            @pl.when(jnp.logical_and(j >= 0, j < p.nch))
            def _():
                rs(j, s).wait_recv()
                at = rows_of(s + 1)
                if s < S - 1:
                    pt[j, at] = pt[j, at] + recvs[s][j]
                    rs(j, s + 1).start()
                else:
                    pg[j, at] = pt[j, at] + recvs[s][j]
                    ag(j, 0).start()

        ia = t - p.vlag * pos

        @pl.when(jnp.logical_and(ia >= 0, ia < p.np))
        def _():
            @pl.when(pos > 0)
            def _():
                ring(ia, 0, va_s, va_r, prv).wait_recv()

            @pl.when(pos < cols - 1)
            def _():
                ring(ia, 0, va_s, va_r, nxt).start()

            cross_core(core, ia, 0, 0).start()

        ib = t - p.vlag * posb

        @pl.when(jnp.logical_and(ib >= 0, ib < p.np))
        def _():
            @pl.when(posb > 0)
            def _():
                ring(ib, half, vb_s, vb_r, nxt).wait_recv()

            @pl.when(posb < cols - 1)
            def _():
                ring(ib, half, vb_s, vb_r, prv).start()

            cross_core(core, ib, half, 1).start()

        @pl.when(t == p.lag)
        def _():
            at = aligned(r * pc, pc)
            total = cx[at]
            for d in range(1, rows):
                cross_sum(d).wait_recv()
                total = total + cr[d]
            cf[at] = total
            for d in range(1, rows):
                cross_all(d).start()

        @pl.when(t == p.gram_tick)
        def _():
            for b in range(2):
                for i in range(p.np):
                    cross_core(1 - core, i, b * half, b).wait_recv()
            pltpu.make_async_copy(vc, vc_hbm, io.at[3]).start()
            at = rows_of(S)

            def part(j, total):
                n0 = aligned((j // 2) * w, w)
                return total + dot3(pg[j, at], vc[j % 2, n0, :])

            gm[...] = lax.fori_loop(0, p.nm, part, jnp.zeros((size[S], p.nb2), F32))
            for d in range(1, cols):
                gram_sum(d).start()

        @pl.when(t == p.gram_tick + p.lag)
        def _():
            total = gm[...]
            for d in range(1, cols):
                gram_sum(d).wait_recv()
                total = total + gr[d]
            gf[rows_of(S)] = total
            for d in range(1, rows):
                gram_all(d).start()

        @pl.when(t == p.gram_tick + 2 * p.lag)
        def _():
            for d in range(1, rows):
                gram_wait(d).wait_recv()
            nb = p.nb
            one, two = f1[...], f2[...]
            cross = cf[...]
            g11, g21, g22 = gf[:nb, :nb], gf[nb:, :nb], gf[nb:, nb:]
            x1 = exact(exact(one, g11, TN), one)
            key = exact(one, g21, ((0,), (1,))) - 0.5 * exact(x1, cross, TN)
            twist = exact(cross, key, TN)
            gram2 = g22 + twist - twist.T
            x2 = exact(exact(two, gram2, TN), two)
            mixed = exact(key + 0.5 * exact(x1, cross), two)
            skw[:nb, :nb] = 0.5 * (x1.T - x1)
            skw[:nb, nb:] = mixed
            skw[nb:, :nb] = -mixed.T
            skw[nb:, nb:] = 0.5 * (x2.T - x2)

        @pl.when(t + 1 < p.nch)
        def _():
            fetch(t + 1)

        @pl.when(t < p.nch)
        def _():
            slot = t % 2
            pltpu.make_async_copy(mbuf.at[slot], mbuf.at[slot], m_in.at[slot]).wait()
            high, low = split(mbuf[slot])
            both = dot(vt[...], high)
            pt[t] = both[: p.nb2] + both[p.nb2 :] + dot(vt[pl.ds(0, p.nb2)], low)
            rs(t, 0).start()

        jn = t + 1 - p.done

        @pl.when(jnp.logical_and(jn >= 0, jn < p.nm))
        def _():
            @pl.when(jn >= 3)
            def _():
                pltpu.make_async_copy(
                    tbuf.at[jn % 3], t_hbm.at[:, pl.ds(column(jn), w)], t_out.at[jn % 3]
                ).wait()

            m_copy(jn, tbuf, jn % 3, t_in.at[jn % 3]).start()

        @pl.when(t == p.done - 1)
        def _():
            for d in range(1, rows):
                cross_got(d).wait_recv()
            nb = p.nb
            comp[:nb, :nb] = f1[...]
            comp[:nb, nb:] = -exact(exact(f1[...], cf[...]), f2[...])
            comp[nb:, :nb] = jnp.zeros((nb, nb), F32)
            comp[nb:, nb:] = f2[...]

            def build(i, _):
                at = aligned(i * step, step)
                high, low = split(dot3(vown[at, :], comp[...], NT))
                lq[0, at] = high
                lq[1, at] = low
                return 0

            lax.fori_loop(0, nblk, build, 0)

        j = t - p.done

        @pl.when(jnp.logical_and(j >= 0, j < p.nm))
        def _():
            slot = j % 3
            m_copy(j, tbuf, slot, t_in.at[slot]).wait()
            high, low = split(pg[j])

            def add(i, _):
                at = aligned(i * step, step)
                lh = lq[0, at]
                tbuf[slot, at] = tbuf[slot, at] - (dot(lh, high) + dot(lq[1, at], high) + dot(lh, low))
                return 0

            lax.fori_loop(0, nblk, add, 0)
            pltpu.make_async_copy(tbuf.at[slot], t_hbm.at[:, pl.ds(column(j), w)], t_out.at[slot]).start()

        @pl.when(jnp.logical_and(j >= p.nm, j < p.nch))
        def _():
            yb[j - p.nm] = dot3(comp[...], pg[j])

        return 0

    lax.fori_loop(0, p.ticks, tick, 0)

    def left(i, _):
        for b in range(w // step):
            at = aligned(i * w + b * step, step)
            mixed = dot3(pr[i, :, pl.ds(b * step, step)].T, comp[...])
            lp[at] = dot3(vown[at, :], skw[...]) - mixed
        return 0

    lax.fori_loop(0, p.nz, left, 0)
    lp_out = pltpu.make_async_copy(lp, lp_hbm, io.at[0])
    lp_out.start()
    outs = []
    for b in range(p.nv):
        copy = pltpu.make_async_copy(yb.at[b], y_hbm.at[:, pl.ds(b * w, w)], io.at[4 + b])
        copy.start()
        outs.append(copy)

    def drain(j, _):
        for s in range(S):
            rs(j, s).wait_send()
            ag(j, s).wait_send()
        return 0

    lax.fori_loop(0, p.nch, drain, 0)

    def drain_z(i, _):
        for s in range(p.nsub):
            @pl.when(jnp.logical_and(c >= q, c < cols - 1))
            def _():
                zcopy(pr.at[i], i, s, zu_s, c + 1).wait_send()

            @pl.when(jnp.logical_and(c <= q, c > 0))
            def _():
                zcopy(pr.at[i], i, s, zd_s, c - 1).wait_send()
        return 0

    lax.fori_loop(0, p.nz, drain_z, 0)

    def drain_v(i, _):
        @pl.when(pos < cols - 1)
        def _():
            ring(i, 0, va_s, va_r, nxt).wait_send()

        @pl.when(posb < cols - 1)
        def _():
            ring(i, half, vb_s, vb_r, prv).wait_send()

        cross_core(core, i, 0, 0).wait_send()
        cross_core(core, i, half, 1).wait_send()
        return 0

    lax.fori_loop(0, p.np, drain_v, 0)
    for d in range(1, rows):
        cross_sum(d).wait_send()
        cross_all(d).wait_send()
        gram_all(d).wait_send()
    for d in range(1, cols):
        gram_sum(d).wait_send()
    for j in range(max(0, p.nm - 3), p.nm):
        pltpu.make_async_copy(tbuf.at[j % 3], t_hbm.at[:, pl.ds(column(j), w)], t_out.at[j % 3]).wait()
    pltpu.make_async_copy(vc, vc_hbm, io.at[3]).wait()
    vj_out.wait()
    lp_out.wait()
    for copy in outs:
        copy.wait()


def exchange(p, matrix, vectors, first, second, factor1, factor2):
    n, nb2, w, S = p.n, p.nb2, p.w, p.stages
    hbm = pl.BlockSpec(memory_space=pl.ANY)
    vmem = pl.BlockSpec(memory_space=pltpu.VMEM)
    dma = pltpu.SemaphoreType.DMA

    def body(*refs):
        ins, rest = refs[:11], refs[11:]
        before, rest = rest[:7], rest[7:]
        recvs, rest = rest[:S], rest[S:]
        kernel(p, *ins, *before, recvs, *rest)

    shape = lambda *s: jax.ShapeDtypeStruct(s, F32)
    scratch = [
        pltpu.VMEM((n, nb2), F32),
        pltpu.VMEM((2 * nb2, n), BF16),
        pltpu.VMEM((2, n, nb2), BF16),
        pltpu.VMEM((2, n, w), F32),
        pltpu.VMEM((3, n, w), F32),
        pltpu.VMEM((p.nch, nb2, w), F32),
        pltpu.VMEM((p.nch, nb2, w), F32),
    ]
    scratch += [pltpu.VMEM((p.nch, nb2 >> (s + 1), w), F32) for s in range(S)]
    scratch += [
        pltpu.VMEM((p.nz, nb2, w), F32),
        pltpu.VMEM((2, n, nb2), F32),
        pltpu.VMEM((n, nb2), F32),
        pltpu.VMEM((p.nv, nb2, w), F32),
        pltpu.VMEM((p.nb, p.nb), F32),
        pltpu.VMEM((p.rows, p.piece, p.nb), F32),
        pltpu.VMEM((p.nb, p.nb), F32),
        pltpu.VMEM((nb2 >> S, nb2), F32),
        pltpu.VMEM((p.cols, nb2 >> S, nb2), F32),
        pltpu.VMEM((nb2, nb2), F32),
        pltpu.VMEM((nb2, nb2), F32),
        pltpu.VMEM((nb2, nb2), F32),
    ]
    scratch += [dma((p.nch, S)) for _ in range(4)]
    scratch += [dma((p.nz, p.nsub)) for _ in range(3)]
    scratch += [dma((p.np,)) for _ in range(4)] + [dma((2, p.np)) for _ in range(2)]
    scratch += [dma((p.rows,)) for _ in range(4)]
    scratch += [dma((p.cols,)) for _ in range(2)] + [dma((p.rows,)) for _ in range(2)]
    scratch += [dma((2,)), dma((3,)), dma((3,)), dma((4 + p.nv,))]
    return pl.pallas_call(
        body,
        out_shape=[shape(n, p.nc), shape(n, nb2), shape(2, n, nb2), shape(nb2, p.kc), shape(n, nb2)],
        in_specs=[hbm] * 4 + [vmem] * 2,
        out_specs=[hbm] * 5,
        scratch_shapes=scratch,
        compiler_params=pltpu.CompilerParams(
            collective_id=0, has_side_effects=True, vmem_limit_bytes=VMEM_BYTES
        ),
        cost_estimate=pl.CostEstimate(
            flops=12 * n * p.nc * nb2, bytes_accessed=12 * n * p.nc, transcendentals=0
        ),
    )(matrix, vectors, first, second, factor1, factor2)


def finish_step(nm, lp_ref, vj_ref, vc_ref, y_ref, t_ref, vec_ref, out_ref, back_ref, left, own):
    step = pl.program_id(0)
    n, nb2 = lp_ref.shape

    @pl.when(step == 0)
    def _():
        def prepare(i, _):
            at = aligned(i * 256, 256)
            for src, dst in ((lp_ref, left), (vj_ref, own)):
                high, low = split(src[at, :])
                dst[at, pl.ds(0, nb2)] = high
                dst[at, pl.ds(nb2, nb2)] = low
                dst[at, pl.ds(2 * nb2, nb2)] = high
            return 0

        lax.fori_loop(0, n // 256, prepare, 0)

    @pl.when(step < nm)
    def _():
        high, low = split(vc_ref[...])
        right = jnp.concatenate([high, high, low], axis=1)
        out_ref[...] = t_ref[...] - dot(left[...], right, NT)

    @pl.when(step >= nm)
    def _():
        high, low = split(y_ref[...])
        right = jnp.concatenate([high, high, low], axis=0)
        back_ref[...] = vec_ref[...] - dot(own[...], right)


def finish(p, partly, left, panel, inner, joined, vectors):
    n, nb2, w = p.n, p.nb2, min(512, p.kc)
    nm, nv = p.nc // w, p.kc // w
    one = lambda i: jnp.minimum(i, nm - 1)
    two = lambda i: jnp.maximum(i - nm, 0)
    whole = pl.BlockSpec((n, nb2), lambda i: (0, 0))
    matrix_block = pl.BlockSpec((n, w), lambda i: (0, one(i)))
    vector_block = pl.BlockSpec((n, w), lambda i: (0, two(i)))
    return pl.pallas_call(
        functools.partial(finish_step, nm),
        grid=(nm + nv,),
        out_shape=[jax.ShapeDtypeStruct((n, p.nc), F32), jax.ShapeDtypeStruct((n, p.kc), F32)],
        in_specs=[
            whole,
            whole,
            pl.BlockSpec((w, nb2), lambda i: (one(i), 0)),
            pl.BlockSpec((nb2, w), lambda i: (0, two(i))),
            matrix_block,
            vector_block,
        ],
        out_specs=[matrix_block, vector_block],
        scratch_shapes=[pltpu.VMEM((n, 3 * nb2), BF16), pltpu.VMEM((n, 3 * nb2), BF16)],
        compiler_params=pltpu.CompilerParams(vmem_limit_bytes=VMEM_BYTES),
    )(left, joined, panel, inner, partly, vectors)


def solution(mesh):
    rows, cols = mesh.shape["row"], mesh.shape["col"]

    def shards(matrix, first, factor1, second, factor2, vectors):
        p = Plan(rows, cols, *matrix.shape, vectors.shape[1], first.shape[1])
        partly, left, panel, inner, joined = exchange(p, matrix, vectors, first, second, factor1, factor2)
        panel = panel.reshape(2 * p.n, 2 * p.nb)
        return tuple(finish(p, partly, left, panel, inner, joined, vectors))

    in_specs = (P("row", "col"), P("row", None), P(), P("row", None), P(), P("row", "col"))
    out_specs = (P("row", "col"), P("row", "col"))
    return jax.shard_map(shards, mesh=mesh, in_specs=in_specs, out_specs=out_specs, check_vma=False)
```

```python
import functools

import jax
import jax.numpy as jnp
from jax import lax
from jax.experimental import pallas as pl
from jax.experimental.pallas import tpu as pltpu
from jax.sharding import PartitionSpec as P

MESH = pl.DeviceIdType.MESH
F32, BF16 = jnp.float32, jnp.bfloat16
NN = ((1,), (0,))
TN = ((0,), (0,))
NT = ((1,), (1,))
VMEM_BYTES = 61 * 2**20


def dot(left, right, dims=NN):
    return lax.dot_general(left, right, (dims, ((), ())), preferred_element_type=F32)


def exact(left, right, dims=NN):
    return lax.dot_general(
        left, right, (dims, ((), ())), precision=lax.Precision.HIGHEST, preferred_element_type=F32
    )


def split(value):
    high = value.astype(BF16)
    return high, (value - high.astype(F32)).astype(BF16)


def dot3(left, right, dims=NN):
    lh, ll = split(left)
    rh, rl = split(right)
    return dot(lh, rh, dims) + dot(ll, rh, dims) + dot(lh, rl, dims)


def pick(index, table):
    return sum(jnp.where(index == i, v, 0) for i, v in enumerate(table))


def aligned(start, size):
    return pl.ds(pl.multiple_of(start, size), size)


class Plan:
    def __init__(self, rows, cols, n, nc, kc, nb):
        self.rows, self.cols, self.n, self.nc, self.kc, self.nb = rows, cols, n, nc, kc, nb
        self.nb2 = 2 * nb
        self.w = min(256, kc, nc // 2)
        self.nm, self.nv = nc // self.w, kc // self.w
        self.nch = self.nm + self.nv
        self.bits = (rows // 2).bit_length() - 1
        self.stages = 1 + self.bits
        self.nz = self.nm // 2
        self.nsub = 2
        self.np = 16
        self.lag, self.zlag, self.vlag, self.vstart = 2, 2, 2, 4
        self.clag = max(1, self.lag - 1)
        self.rs_at = [self.clag + self.lag * s for s in range(self.stages)]
        self.ag_at = [self.rs_at[-1] + self.lag * (a + 1) for a in range(self.stages - 1)]
        self.ag_at.append(self.ag_at[-1] + self.clag)
        self.gram_tick = max(self.nm + self.rs_at[-1], self.vstart + self.np + self.vlag * (cols - 1))
        self.done = self.ag_at[-1]
        self.ticks = max(
            self.nm + self.done + self.zlag * (cols - 1),
            self.nch + self.done,
            self.gram_tick + 2 * self.lag + 1,
        )
        self.piece = nb // rows


def kernel(
    p,
    m_hbm, vec_hbm, v1_hbm, v2_hbm, f1, f2,
    t_hbm, lp_hbm, vc_hbm, y_hbm, vj_hbm,
    vown, vt, lq, mbuf, tbuf, pt, pg, recvs, pr, vc, lp, yb,
    cx, cr, cf, gm, gr, gf, comp, skw,
    rs_s, rs_r, ag_s, ag_r, zu_s, zd_s, z_r, va_s, va_r, vb_s, vb_r, vx_s, vx_r,
    c1_s, c1_r, c2_s, c2_r, g1_s, g1_r, g2_s, g2_r, m_in, t_in, t_out, io,
):
    r, c = lax.axis_index("row"), lax.axis_index("col")
    rows, cols, w, S = p.rows, p.cols, p.w, p.stages
    core = r % 2
    q = r // 2

    def remote(src, dst, ssem, rsem, row, col):
        return pltpu.make_async_remote_copy(
            src_ref=src, dst_ref=dst, send_sem=ssem, recv_sem=rsem, device_id=(row, col), device_id_type=MESH
        )

    barrier = pltpu.get_barrier_semaphore()
    for d in range(1, rows):
        pl.semaphore_signal(barrier, inc=1, device_id=((r + d) % rows, c), device_id_type=MESH)
    for d in range(1, cols):
        pl.semaphore_signal(barrier, inc=1, device_id=(r, (c + d) % cols), device_id_type=MESH)

    def flip(bit):
        return r + bit * (1 - 2 * ((r // bit) % 2)), (r // bit) % 2

    partner, mine = [], []
    for s in range(S):
        if s == 0:
            who, bit = flip(1)
        else:
            a, abit = flip(1 << s)
            b, bbit = flip(1 << (s % p.bits + 1))
            who, bit = a + core * (b - a), abit + core * (bbit - abit)
        partner.append(who)
        mine.append(bit)
    size = [p.nb2 >> s for s in range(S + 1)]
    off = [0]
    for s in range(S):
        off.append(off[s] + mine[s] * size[s + 1])

    def rows_of(s):
        return aligned(off[s], size[s]) if s else pl.ds(0, size[0])

    def other_rows(s):
        return aligned(off[s] + (1 - mine[s]) * size[s + 1], size[s + 1])

    gray = [i ^ (i >> 1) for i in range(cols)]
    back = [gray.index(i) for i in range(cols)]
    place = pick(q, back)
    pos = (place - pick(c, back) + cols) % cols
    nxt = 2 * pick((place + 1) % cols, gray) + core
    prv = 2 * pick((place + cols - 1) % cols, gray) + core
    posb = (cols - pos) % cols
    hops = jnp.where(c > q, c - q, q - c)

    def column(j):
        return pl.multiple_of((j % 2) * (p.nc // 2) + (j // 2) * w, w)

    def m_copy(j, buf, slot, sem):
        return pltpu.make_async_copy(m_hbm.at[:, pl.ds(column(j), w)], buf.at[slot], sem)

    def v_copy(j, slot):
        return pltpu.make_async_copy(
            vec_hbm.at[:, aligned((j - p.nm) * w, w)], mbuf.at[slot], m_in.at[slot]
        )

    def fetch(j):
        @pl.when(j < p.nm)
        def _():
            m_copy(j, mbuf, j % 2, m_in.at[j % 2]).start()

        @pl.when(jnp.logical_and(j >= p.nm, j < p.nch))
        def _():
            v_copy(j, j % 2).start()

    own1 = pltpu.make_async_copy(v1_hbm, vown.at[:, pl.ds(0, p.nb)], io.at[0])
    own2 = pltpu.make_async_copy(v2_hbm, vown.at[:, pl.ds(p.nb, p.nb)], io.at[1])
    own1.start()
    own2.start()
    m_copy(0, mbuf, 0, m_in.at[0]).start()
    own1.wait()
    own2.wait()
    vj_out = pltpu.make_async_copy(vown, vj_hbm, io.at[2])
    vj_out.start()
    step = 256
    nblk = p.n // step

    def prepare(i, _):
        at = aligned(i * step, step)
        high, low = split(vown[at, :].T)
        vt[pl.ds(0, p.nb2), at] = high
        vt[pl.ds(p.nb2, p.nb2), at] = low
        return 0

    lax.fori_loop(0, nblk, prepare, 0)

    @pl.when(pos == 0)
    def _():
        vc[core] = vown[...]

    def cross_part(i, total):
        at = aligned(i * step, step)
        x2h, x2l = split(vown[at, pl.ds(p.nb, p.nb)])
        th, tl = vt[pl.ds(0, p.nb), at], vt[pl.ds(p.nb2, p.nb), at]
        return total + (dot(th, x2h) + dot(tl, x2h) + dot(th, x2l))

    cx[...] = lax.fori_loop(0, nblk, cross_part, jnp.zeros((p.nb, p.nb), F32))

    pl.semaphore_wait(barrier, rows - 1 + cols - 1)

    pc = p.piece

    def cross_sum(d):
        to = (r + d) % rows
        return remote(cx.at[aligned(to * pc, pc)], cr.at[d], c1_s.at[d], c1_r.at[d], to, c)

    def cross_all(d):
        to = (r + d) % rows
        at = aligned(r * pc, pc)
        return remote(cf.at[at], cf.at[at], c2_s.at[d], c2_r.at[d], to, c)

    def cross_got(d):
        frm = (r + rows - d) % rows
        at = aligned(frm * pc, pc)
        return remote(cf.at[at], cf.at[at], c2_s.at[d], c2_r.at[d], frm, c)

    for d in range(1, rows):
        cross_sum(d).start()

    def rs(j, s):
        return remote(pt.at[j, other_rows(s)], recvs[s].at[j], rs_s.at[j, s], rs_r.at[j, s], partner[s], c)

    def ag(j, a):
        s = S - 1 - a
        at = rows_of(s + 1)
        return remote(pg.at[j, at], pg.at[j, at], ag_s.at[j, a], ag_r.at[j, a], partner[s], c)

    def ag_got(j, a):
        s = S - 1 - a
        at = other_rows(s)
        return remote(pg.at[j, at], pg.at[j, at], ag_s.at[j, a], ag_r.at[j, a], partner[s], c)

    sub = p.nb2 // p.nsub

    def zcopy(src, i, s, sems, to):
        at = aligned(s * sub, sub)
        return remote(src.at[at], pr.at[i, at], sems.at[i, s], z_r.at[i, s], r, to)

    half = p.n // 2
    vpc = half // p.np

    def ring(i, base, ssem, rsem, to):
        at = aligned(base + i * vpc, vpc)
        return remote(vc.at[core, at], vc.at[core, at], ssem.at[i], rsem.at[i], to, c)

    def cross_core(which, i, base, b):
        at = aligned(base + i * vpc, vpc)
        return remote(vc.at[which, at], vc.at[which, at], vx_s.at[b, i], vx_r.at[b, i], partner[0], c)

    def gram_sum(d):
        to = (c + d) % cols
        return remote(gm, gr.at[d], g1_s.at[d], g1_r.at[d], r, to)

    def gram_all(d):
        at = rows_of(S)
        return remote(gf.at[at], gf.at[at], g2_s.at[d], g2_r.at[d], (r + d) % rows, c)

    def gram_wait(d):
        at = rows_of(S)
        return remote(gf.at[at], gf.at[at], g2_s.at[d], g2_r.at[d], (r + d) % rows, c)

    def tick(t, _):
        for a in range(S - 1, -1, -1):
            j = t - p.ag_at[a]

            @pl.when(jnp.logical_and(j >= 0, j < p.nch))
            def _():
                ag_got(j, a).wait_recv()
                if a < S - 1:
                    ag(j, a + 1).start()

        j = t - p.done

        @pl.when(jnp.logical_and(jnp.logical_and(j >= 0, j < p.nm), jnp.logical_and(j % 2 == core, c == q)))
        def _():
            i = j // 2
            for s in range(p.nsub):
                @pl.when(c < cols - 1)
                def _():
                    zcopy(pg.at[j], i, s, zu_s, c + 1).start()

                @pl.when(c > 0)
                def _():
                    zcopy(pg.at[j], i, s, zd_s, c - 1).start()
            pr[i] = pg[j]

        j = t - p.done - p.zlag * hops

        @pl.when(jnp.logical_and(jnp.logical_and(j >= 0, j < p.nm), jnp.logical_and(j % 2 == core, c != q)))
        def _():
            i = j // 2
            for s in range(p.nsub):
                zcopy(pr.at[i], i, s, zu_s, c).wait_recv()

                @pl.when(jnp.logical_and(c > q, c < cols - 1))
                def _():
                    zcopy(pr.at[i], i, s, zu_s, c + 1).start()

                @pl.when(jnp.logical_and(c < q, c > 0))
                def _():
                    zcopy(pr.at[i], i, s, zd_s, c - 1).start()

        for s in range(S - 1, -1, -1):
            j = t - p.rs_at[s]

            @pl.when(jnp.logical_and(j >= 0, j < p.nch))
            def _():
                rs(j, s).wait_recv()
                at = rows_of(s + 1)
                if s < S - 1:
                    pt[j, at] = pt[j, at] + recvs[s][j]
                    rs(j, s + 1).start()
                else:
                    pg[j, at] = pt[j, at] + recvs[s][j]
                    ag(j, 0).start()

        ia = t - p.vstart - p.vlag * pos

        @pl.when(jnp.logical_and(ia >= 0, ia < p.np))
        def _():
            @pl.when(pos > 0)
            def _():
                ring(ia, 0, va_s, va_r, prv).wait_recv()

            @pl.when(pos < cols - 1)
            def _():
                ring(ia, 0, va_s, va_r, nxt).start()

            cross_core(core, ia, 0, 0).start()

        ib = t - p.vstart - p.vlag * posb

        @pl.when(jnp.logical_and(ib >= 0, ib < p.np))
        def _():
            @pl.when(posb > 0)
            def _():
                ring(ib, half, vb_s, vb_r, nxt).wait_recv()

            @pl.when(posb < cols - 1)
            def _():
                ring(ib, half, vb_s, vb_r, prv).start()

            cross_core(core, ib, half, 1).start()

        @pl.when(t == p.lag)
        def _():
            at = aligned(r * pc, pc)
            total = cx[at]
            for d in range(1, rows):
                cross_sum(d).wait_recv()
                total = total + cr[d]
            cf[at] = total
            for d in range(1, rows):
                cross_all(d).start()

        @pl.when(t == p.gram_tick)
        def _():
            for b in range(2):
                for i in range(p.np):
                    cross_core(1 - core, i, b * half, b).wait_recv()
            pltpu.make_async_copy(vc, vc_hbm, io.at[3]).start()
            at = rows_of(S)

            def part(j, total):
                n0 = aligned((j // 2) * w, w)
                return total + dot3(pg[j, at], vc[j % 2, n0, :])

            gm[...] = lax.fori_loop(0, p.nm, part, jnp.zeros((size[S], p.nb2), F32))
            for d in range(1, cols):
                gram_sum(d).start()

        @pl.when(t == p.gram_tick + p.lag)
        def _():
            total = gm[...]
            for d in range(1, cols):
                gram_sum(d).wait_recv()
                total = total + gr[d]
            gf[rows_of(S)] = total
            for d in range(1, rows):
                gram_all(d).start()

        @pl.when(t == p.gram_tick + 2 * p.lag)
        def _():
            for d in range(1, rows):
                gram_wait(d).wait_recv()
            nb = p.nb
            one, two = f1[...], f2[...]
            cross = cf[...]
            g11, g21, g22 = gf[:nb, :nb], gf[nb:, :nb], gf[nb:, nb:]
            x1 = exact(exact(one, g11, TN), one)
            key = exact(one, g21, ((0,), (1,))) - 0.5 * exact(x1, cross, TN)
            twist = exact(cross, key, TN)
            gram2 = g22 + twist - twist.T
            x2 = exact(exact(two, gram2, TN), two)
            mixed = exact(key + 0.5 * exact(x1, cross), two)
            skw[:nb, :nb] = 0.5 * (x1.T - x1)
            skw[:nb, nb:] = mixed
            skw[nb:, :nb] = -mixed.T
            skw[nb:, nb:] = 0.5 * (x2.T - x2)

        @pl.when(t + 1 < p.nch)
        def _():
            fetch(t + 1)

        @pl.when(t < p.nch)
        def _():
            slot = t % 2
            pltpu.make_async_copy(mbuf.at[slot], mbuf.at[slot], m_in.at[slot]).wait()
            high, low = split(mbuf[slot])
            both = dot(vt[...], high)
            pt[t] = both[: p.nb2] + both[p.nb2 :] + dot(vt[pl.ds(0, p.nb2)], low)
            rs(t, 0).start()

        jn = t + 1 - p.done

        @pl.when(jnp.logical_and(jn >= 0, jn < p.nm))
        def _():
            @pl.when(jn >= 3)
            def _():
                pltpu.make_async_copy(
                    tbuf.at[jn % 3], t_hbm.at[:, pl.ds(column(jn), w)], t_out.at[jn % 3]
                ).wait()

            m_copy(jn, tbuf, jn % 3, t_in.at[jn % 3]).start()

        @pl.when(t == p.done - 1)
        def _():
            for d in range(1, rows):
                cross_got(d).wait_recv()
            nb = p.nb
            comp[:nb, :nb] = f1[...]
            comp[:nb, nb:] = -exact(exact(f1[...], cf[...]), f2[...])
            comp[nb:, :nb] = jnp.zeros((nb, nb), F32)
            comp[nb:, nb:] = f2[...]

            def build(i, _):
                at = aligned(i * step, step)
                high, low = split(dot3(vown[at, :], comp[...], NT))
                lq[0, at] = high
                lq[1, at] = low
                return 0

            lax.fori_loop(0, nblk, build, 0)

        j = t - p.done

        @pl.when(jnp.logical_and(j >= 0, j < p.nm))
        def _():
            slot = j % 3
            m_copy(j, tbuf, slot, t_in.at[slot]).wait()
            high, low = split(pg[j])

            def add(i, _):
                at = aligned(i * step, step)
                lh = lq[0, at]
                tbuf[slot, at] = tbuf[slot, at] - (dot(lh, high) + dot(lq[1, at], high) + dot(lh, low))
                return 0

            lax.fori_loop(0, nblk, add, 0)
            pltpu.make_async_copy(tbuf.at[slot], t_hbm.at[:, pl.ds(column(j), w)], t_out.at[slot]).start()

        @pl.when(jnp.logical_and(j >= p.nm, j < p.nch))
        def _():
            yb[j - p.nm] = dot3(comp[...], pg[j])

        return 0

    lax.fori_loop(0, p.ticks, tick, 0)

    def left(i, _):
        for b in range(w // step):
            at = aligned(i * w + b * step, step)
            mixed = dot3(pr[i, :, pl.ds(b * step, step)].T, comp[...])
            lp[at] = dot3(vown[at, :], skw[...]) - mixed
        return 0

    lax.fori_loop(0, p.nz, left, 0)
    lp_out = pltpu.make_async_copy(lp, lp_hbm, io.at[0])
    lp_out.start()
    outs = []
    for b in range(p.nv):
        copy = pltpu.make_async_copy(yb.at[b], y_hbm.at[:, pl.ds(b * w, w)], io.at[4 + b])
        copy.start()
        outs.append(copy)

    def drain(j, _):
        for s in range(S):
            rs(j, s).wait_send()
            ag(j, s).wait_send()
        return 0

    lax.fori_loop(0, p.nch, drain, 0)

    def drain_z(i, _):
        for s in range(p.nsub):
            @pl.when(jnp.logical_and(c >= q, c < cols - 1))
            def _():
                zcopy(pr.at[i], i, s, zu_s, c + 1).wait_send()

            @pl.when(jnp.logical_and(c <= q, c > 0))
            def _():
                zcopy(pr.at[i], i, s, zd_s, c - 1).wait_send()
        return 0

    lax.fori_loop(0, p.nz, drain_z, 0)

    def drain_v(i, _):
        @pl.when(pos < cols - 1)
        def _():
            ring(i, 0, va_s, va_r, nxt).wait_send()

        @pl.when(posb < cols - 1)
        def _():
            ring(i, half, vb_s, vb_r, prv).wait_send()

        cross_core(core, i, 0, 0).wait_send()
        cross_core(core, i, half, 1).wait_send()
        return 0

    lax.fori_loop(0, p.np, drain_v, 0)
    for d in range(1, rows):
        cross_sum(d).wait_send()
        cross_all(d).wait_send()
        gram_all(d).wait_send()
    for d in range(1, cols):
        gram_sum(d).wait_send()
    for j in range(max(0, p.nm - 3), p.nm):
        pltpu.make_async_copy(tbuf.at[j % 3], t_hbm.at[:, pl.ds(column(j), w)], t_out.at[j % 3]).wait()
    pltpu.make_async_copy(vc, vc_hbm, io.at[3]).wait()
    vj_out.wait()
    lp_out.wait()
    for copy in outs:
        copy.wait()


def exchange(p, matrix, vectors, first, second, factor1, factor2):
    n, nb2, w, S = p.n, p.nb2, p.w, p.stages
    hbm = pl.BlockSpec(memory_space=pl.ANY)
    vmem = pl.BlockSpec(memory_space=pltpu.VMEM)
    dma = pltpu.SemaphoreType.DMA

    def body(*refs):
        ins, rest = refs[:11], refs[11:]
        before, rest = rest[:7], rest[7:]
        recvs, rest = rest[:S], rest[S:]
        kernel(p, *ins, *before, recvs, *rest)

    shape = lambda *s: jax.ShapeDtypeStruct(s, F32)
    scratch = [
        pltpu.VMEM((n, nb2), F32),
        pltpu.VMEM((2 * nb2, n), BF16),
        pltpu.VMEM((2, n, nb2), BF16),
        pltpu.VMEM((2, n, w), F32),
        pltpu.VMEM((3, n, w), F32),
        pltpu.VMEM((p.nch, nb2, w), F32),
        pltpu.VMEM((p.nch, nb2, w), F32),
    ]
    scratch += [pltpu.VMEM((p.nch, nb2 >> (s + 1), w), F32) for s in range(S)]
    scratch += [
        pltpu.VMEM((p.nz, nb2, w), F32),
        pltpu.VMEM((2, n, nb2), F32),
        pltpu.VMEM((n, nb2), F32),
        pltpu.VMEM((p.nv, nb2, w), F32),
        pltpu.VMEM((p.nb, p.nb), F32),
        pltpu.VMEM((p.rows, p.piece, p.nb), F32),
        pltpu.VMEM((p.nb, p.nb), F32),
        pltpu.VMEM((nb2 >> S, nb2), F32),
        pltpu.VMEM((p.cols, nb2 >> S, nb2), F32),
        pltpu.VMEM((nb2, nb2), F32),
        pltpu.VMEM((nb2, nb2), F32),
        pltpu.VMEM((nb2, nb2), F32),
    ]
    scratch += [dma((p.nch, S)) for _ in range(4)]
    scratch += [dma((p.nz, p.nsub)) for _ in range(3)]
    scratch += [dma((p.np,)) for _ in range(4)] + [dma((2, p.np)) for _ in range(2)]
    scratch += [dma((p.rows,)) for _ in range(4)]
    scratch += [dma((p.cols,)) for _ in range(2)] + [dma((p.rows,)) for _ in range(2)]
    scratch += [dma((2,)), dma((3,)), dma((3,)), dma((4 + p.nv,))]
    return pl.pallas_call(
        body,
        out_shape=[shape(n, p.nc), shape(n, nb2), shape(2, n, nb2), shape(nb2, p.kc), shape(n, nb2)],
        in_specs=[hbm] * 4 + [vmem] * 2,
        out_specs=[hbm] * 5,
        scratch_shapes=scratch,
        compiler_params=pltpu.CompilerParams(
            collective_id=0, has_side_effects=True, vmem_limit_bytes=VMEM_BYTES
        ),
        cost_estimate=pl.CostEstimate(
            flops=12 * n * p.nc * nb2, bytes_accessed=12 * n * p.nc, transcendentals=0
        ),
    )(matrix, vectors, first, second, factor1, factor2)


def finish_step(nm, lp_ref, vj_ref, vc_ref, y_ref, t_ref, vec_ref, out_ref, back_ref, left, own):
    step = pl.program_id(0)
    n, nb2 = lp_ref.shape

    @pl.when(step == 0)
    def _():
        def prepare(i, _):
            at = aligned(i * 256, 256)
            for src, dst in ((lp_ref, left), (vj_ref, own)):
                high, low = split(src[at, :])
                dst[at, pl.ds(0, nb2)] = high
                dst[at, pl.ds(nb2, nb2)] = low
                dst[at, pl.ds(2 * nb2, nb2)] = high
            return 0

        lax.fori_loop(0, n // 256, prepare, 0)

    @pl.when(step < nm)
    def _():
        high, low = split(vc_ref[...])
        right = jnp.concatenate([high, high, low], axis=1)
        out_ref[...] = t_ref[...] - dot(left[...], right, NT)

    @pl.when(step >= nm)
    def _():
        high, low = split(y_ref[...])
        right = jnp.concatenate([high, high, low], axis=0)
        back_ref[...] = vec_ref[...] - dot(own[...], right)


def finish(p, partly, left, panel, inner, joined, vectors):
    n, nb2, w = p.n, p.nb2, min(512, p.kc)
    nm, nv = p.nc // w, p.kc // w
    one = lambda i: jnp.minimum(i, nm - 1)
    two = lambda i: jnp.maximum(i - nm, 0)
    whole = pl.BlockSpec((n, nb2), lambda i: (0, 0))
    matrix_block = pl.BlockSpec((n, w), lambda i: (0, one(i)))
    vector_block = pl.BlockSpec((n, w), lambda i: (0, two(i)))
    return pl.pallas_call(
        functools.partial(finish_step, nm),
        grid=(nm + nv,),
        out_shape=[jax.ShapeDtypeStruct((n, p.nc), F32), jax.ShapeDtypeStruct((n, p.kc), F32)],
        in_specs=[
            whole,
            whole,
            pl.BlockSpec((w, nb2), lambda i: (one(i), 0)),
            pl.BlockSpec((nb2, w), lambda i: (0, two(i))),
            matrix_block,
            vector_block,
        ],
        out_specs=[matrix_block, vector_block],
        scratch_shapes=[pltpu.VMEM((n, 3 * nb2), BF16), pltpu.VMEM((n, 3 * nb2), BF16)],
        compiler_params=pltpu.CompilerParams(vmem_limit_bytes=VMEM_BYTES),
    )(left, joined, panel, inner, partly, vectors)


def solution(mesh):
    rows, cols = mesh.shape["row"], mesh.shape["col"]

    def shards(matrix, first, factor1, second, factor2, vectors):
        p = Plan(rows, cols, *matrix.shape, vectors.shape[1], first.shape[1])
        partly, left, panel, inner, joined = exchange(p, matrix, vectors, first, second, factor1, factor2)
        panel = panel.reshape(2 * p.n, 2 * p.nb)
        return tuple(finish(p, partly, left, panel, inner, joined, vectors))

    in_specs = (P("row", "col"), P("row", None), P(), P("row", None), P(), P("row", "col"))
    out_specs = (P("row", "col"), P("row", "col"))
    return jax.shard_map(shards, mesh=mesh, in_specs=in_specs, out_specs=out_specs, check_vma=False)
```

```python
import functools

import jax
import jax.numpy as jnp
from jax import lax
from jax.experimental import pallas as pl
from jax.experimental.pallas import tpu as pltpu
from jax.sharding import PartitionSpec as P

MESH = pl.DeviceIdType.MESH
F32, BF16 = jnp.float32, jnp.bfloat16
NN = ((1,), (0,))
TN = ((0,), (0,))
NT = ((1,), (1,))
VMEM_BYTES = 61 * 2**20


def dot(left, right, dims=NN):
    return lax.dot_general(left, right, (dims, ((), ())), preferred_element_type=F32)


def exact(left, right, dims=NN):
    return lax.dot_general(
        left, right, (dims, ((), ())), precision=lax.Precision.HIGHEST, preferred_element_type=F32
    )


def split(value):
    high = value.astype(BF16)
    return high, (value - high.astype(F32)).astype(BF16)


def dot3(left, right, dims=NN):
    lh, ll = split(left)
    rh, rl = split(right)
    return dot(lh, rh, dims) + dot(ll, rh, dims) + dot(lh, rl, dims)


def pick(index, table):
    return sum(jnp.where(index == i, v, 0) for i, v in enumerate(table))


def aligned(start, size):
    return pl.ds(pl.multiple_of(start, size), size)


class Plan:
    def __init__(self, rows, cols, n, nc, kc, nb):
        self.rows, self.cols, self.n, self.nc, self.kc, self.nb = rows, cols, n, nc, kc, nb
        self.nb2 = 2 * nb
        self.w = min(256, kc, nc // 2)
        self.nm, self.nv = nc // self.w, kc // self.w
        self.nch = self.nm + self.nv
        self.bits = (rows // 2).bit_length() - 1
        self.stages = 1 + self.bits
        self.nz = self.nm // 2
        self.nsub = 2
        self.np = 16
        self.lag, self.zlag, self.vlag, self.vstart = 2, 2, 2, 4
        self.clag = max(1, self.lag - 1)
        self.rs_at = [self.clag + self.lag * s for s in range(self.stages)]
        self.ag_at = [self.rs_at[-1] + self.lag * (a + 1) for a in range(self.stages - 1)]
        self.ag_at.append(self.ag_at[-1] + self.clag)
        self.gram_tick = max(self.nm + self.rs_at[-1], self.vstart + self.np + self.vlag * (cols - 1))
        self.done = self.ag_at[-1]
        self.ticks = max(
            self.nm + self.done + self.zlag * (cols - 1),
            self.nch + self.done,
            self.gram_tick + 2 * self.lag + 1,
        )
        self.piece = nb // rows


def kernel(
    p,
    m_hbm, vec_hbm, v1_hbm, v2_hbm, f1, f2,
    t_hbm, lp_hbm, vc_hbm, y_hbm, vj_hbm,
    vown, vt, lq, mbuf, tbuf, pt, pg, recvs, pr, vc, lp, yb,
    cx, cr, cf, gm, gr, gf, comp, skw,
    rs_s, rs_r, ag_s, ag_r, zu_s, zd_s, z_r, va_s, va_r, vb_s, vb_r, vx_s, vx_r,
    c1_s, c1_r, c2_s, c2_r, g1_s, g1_r, g2_s, g2_r, m_in, t_in, t_out, io,
):
    r, c = lax.axis_index("row"), lax.axis_index("col")
    rows, cols, w, S = p.rows, p.cols, p.w, p.stages
    core = r % 2
    q = r // 2

    def remote(src, dst, ssem, rsem, row, col):
        return pltpu.make_async_remote_copy(
            src_ref=src, dst_ref=dst, send_sem=ssem, recv_sem=rsem, device_id=(row, col), device_id_type=MESH
        )

    barrier = pltpu.get_barrier_semaphore()
    for d in range(1, rows):
        pl.semaphore_signal(barrier, inc=1, device_id=((r + d) % rows, c), device_id_type=MESH)
    for d in range(1, cols):
        pl.semaphore_signal(barrier, inc=1, device_id=(r, (c + d) % cols), device_id_type=MESH)

    def flip(bit):
        return r + bit * (1 - 2 * ((r // bit) % 2)), (r // bit) % 2

    partner, mine = [], []
    for s in range(S):
        if s == 0:
            who, bit = flip(1)
        else:
            a, abit = flip(1 << s)
            b, bbit = flip(1 << (s % p.bits + 1))
            who, bit = a + core * (b - a), abit + core * (bbit - abit)
        partner.append(who)
        mine.append(bit)
    size = [p.nb2 >> s for s in range(S + 1)]
    off = [0]
    for s in range(S):
        off.append(off[s] + mine[s] * size[s + 1])

    def rows_of(s):
        return aligned(off[s], size[s]) if s else pl.ds(0, size[0])

    def other_rows(s):
        return aligned(off[s] + (1 - mine[s]) * size[s + 1], size[s + 1])

    gray = [i ^ (i >> 1) for i in range(cols)]
    back = [gray.index(i) for i in range(cols)]
    place = pick(q, back)
    pos = (place - pick(c, back) + cols) % cols
    nxt = 2 * pick((place + 1) % cols, gray) + core
    prv = 2 * pick((place + cols - 1) % cols, gray) + core
    posb = (cols - pos) % cols
    hops = jnp.where(c > q, c - q, q - c)

    def column(j):
        return pl.multiple_of((j % 2) * (p.nc // 2) + (j // 2) * w, w)

    def m_copy(j, buf, slot, sem):
        return pltpu.make_async_copy(m_hbm.at[:, pl.ds(column(j), w)], buf.at[slot], sem)

    def v_copy(j, slot):
        return pltpu.make_async_copy(
            vec_hbm.at[:, aligned((j - p.nm) * w, w)], mbuf.at[slot], m_in.at[slot]
        )

    def fetch(j):
        @pl.when(j < p.nm)
        def _():
            m_copy(j, mbuf, j % 2, m_in.at[j % 2]).start()

        @pl.when(jnp.logical_and(j >= p.nm, j < p.nch))
        def _():
            v_copy(j, j % 2).start()

    own1 = pltpu.make_async_copy(v1_hbm, vown.at[:, pl.ds(0, p.nb)], io.at[0])
    own2 = pltpu.make_async_copy(v2_hbm, vown.at[:, pl.ds(p.nb, p.nb)], io.at[1])
    own1.start()
    own2.start()
    m_copy(0, mbuf, 0, m_in.at[0]).start()
    own1.wait()
    own2.wait()
    vj_out = pltpu.make_async_copy(vown, vj_hbm, io.at[2])
    vj_out.start()
    step = 256
    nblk = p.n // step

    def prepare(i, _):
        at = aligned(i * step, step)
        high, low = split(vown[at, :].T)
        vt[pl.ds(0, p.nb2), at] = high
        vt[pl.ds(p.nb2, p.nb2), at] = low
        return 0

    lax.fori_loop(0, nblk, prepare, 0)

    @pl.when(pos == 0)
    def _():
        vc[core] = vown[...]

    def cross_part(i, total):
        at = aligned(i * step, step)
        x2h, x2l = split(vown[at, pl.ds(p.nb, p.nb)])
        th, tl = vt[pl.ds(0, p.nb), at], vt[pl.ds(p.nb2, p.nb), at]
        return total + (dot(th, x2h) + dot(tl, x2h) + dot(th, x2l))

    cx[...] = lax.fori_loop(0, nblk, cross_part, jnp.zeros((p.nb, p.nb), F32))

    pl.semaphore_wait(barrier, rows - 1 + cols - 1)

    pc = p.piece

    def cross_sum(d):
        to = (r + d) % rows
        return remote(cx.at[aligned(to * pc, pc)], cr.at[d], c1_s.at[d], c1_r.at[d], to, c)

    def cross_all(d):
        to = (r + d) % rows
        at = aligned(r * pc, pc)
        return remote(cf.at[at], cf.at[at], c2_s.at[d], c2_r.at[d], to, c)

    def cross_got(d):
        frm = (r + rows - d) % rows
        at = aligned(frm * pc, pc)
        return remote(cf.at[at], cf.at[at], c2_s.at[d], c2_r.at[d], frm, c)

    for d in range(1, rows):
        cross_sum(d).start()

    def rs(j, s):
        return remote(pt.at[j, other_rows(s)], recvs[s].at[j], rs_s.at[j, s], rs_r.at[j, s], partner[s], c)

    def ag(j, a):
        s = S - 1 - a
        at = rows_of(s + 1)
        return remote(pg.at[j, at], pg.at[j, at], ag_s.at[j, a], ag_r.at[j, a], partner[s], c)

    def ag_got(j, a):
        s = S - 1 - a
        at = other_rows(s)
        return remote(pg.at[j, at], pg.at[j, at], ag_s.at[j, a], ag_r.at[j, a], partner[s], c)

    sub = p.nb2 // p.nsub

    def zcopy(src, i, s, sems, to):
        at = aligned(s * sub, sub)
        return remote(src.at[at], pr.at[i, at], sems.at[i, s], z_r.at[i, s], r, to)

    half = p.n // 2
    vpc = half // p.np

    def ring(i, base, ssem, rsem, to):
        at = aligned(base + i * vpc, vpc)
        return remote(vc.at[core, at], vc.at[core, at], ssem.at[i], rsem.at[i], to, c)

    def cross_core(which, i, base, b):
        at = aligned(base + i * vpc, vpc)
        return remote(vc.at[which, at], vc.at[which, at], vx_s.at[b, i], vx_r.at[b, i], partner[0], c)

    def gram_sum(d):
        to = (c + d) % cols
        return remote(gm, gr.at[d], g1_s.at[d], g1_r.at[d], r, to)

    def gram_all(d):
        at = rows_of(S)
        return remote(gf.at[at], gf.at[at], g2_s.at[d], g2_r.at[d], (r + d) % rows, c)

    def gram_wait(d):
        at = rows_of(S)
        return remote(gf.at[at], gf.at[at], g2_s.at[d], g2_r.at[d], (r + d) % rows, c)

    def tick(t, _):
        for a in range(S - 1, -1, -1):
            j = t - p.ag_at[a]

            @pl.when(jnp.logical_and(j >= 0, j < p.nch))
            def _():
                ag_got(j, a).wait_recv()
                if a < S - 1:
                    ag(j, a + 1).start()

        j = t - p.done

        @pl.when(jnp.logical_and(jnp.logical_and(j >= 0, j < p.nm), jnp.logical_and(j % 2 == core, c == q)))
        def _():
            i = j // 2
            for s in range(p.nsub):
                @pl.when(c < cols - 1)
                def _():
                    zcopy(pg.at[j], i, s, zu_s, c + 1).start()

                @pl.when(c > 0)
                def _():
                    zcopy(pg.at[j], i, s, zd_s, c - 1).start()
            pr[i] = pg[j]

        j = t - p.done - p.zlag * hops

        @pl.when(jnp.logical_and(jnp.logical_and(j >= 0, j < p.nm), jnp.logical_and(j % 2 == core, c != q)))
        def _():
            i = j // 2
            for s in range(p.nsub):
                zcopy(pr.at[i], i, s, zu_s, c).wait_recv()

                @pl.when(jnp.logical_and(c > q, c < cols - 1))
                def _():
                    zcopy(pr.at[i], i, s, zu_s, c + 1).start()

                @pl.when(jnp.logical_and(c < q, c > 0))
                def _():
                    zcopy(pr.at[i], i, s, zd_s, c - 1).start()

        for s in range(S - 1, -1, -1):
            j = t - p.rs_at[s]

            @pl.when(jnp.logical_and(j >= 0, j < p.nch))
            def _():
                rs(j, s).wait_recv()
                at = rows_of(s + 1)
                if s < S - 1:
                    pt[j, at] = pt[j, at] + recvs[s][j]
                    rs(j, s + 1).start()
                else:
                    pg[j, at] = pt[j, at] + recvs[s][j]
                    ag(j, 0).start()

        ia = t - p.vstart - p.vlag * pos

        @pl.when(jnp.logical_and(ia >= 0, ia < p.np))
        def _():
            @pl.when(pos > 0)
            def _():
                ring(ia, 0, va_s, va_r, prv).wait_recv()

            @pl.when(pos < cols - 1)
            def _():
                ring(ia, 0, va_s, va_r, nxt).start()

            cross_core(core, ia, 0, 0).start()

        ib = t - p.vstart - p.vlag * posb

        @pl.when(jnp.logical_and(ib >= 0, ib < p.np))
        def _():
            @pl.when(posb > 0)
            def _():
                ring(ib, half, vb_s, vb_r, nxt).wait_recv()

            @pl.when(posb < cols - 1)
            def _():
                ring(ib, half, vb_s, vb_r, prv).start()

            cross_core(core, ib, half, 1).start()

        @pl.when(t == p.lag)
        def _():
            at = aligned(r * pc, pc)
            total = cx[at]
            for d in range(1, rows):
                cross_sum(d).wait_recv()
                total = total + cr[d]
            cf[at] = total
            for d in range(1, rows):
                cross_all(d).start()

        @pl.when(t == p.gram_tick)
        def _():
            for b in range(2):
                for i in range(p.np):
                    cross_core(1 - core, i, b * half, b).wait_recv()
            pltpu.make_async_copy(vc, vc_hbm, io.at[3]).start()
            at = rows_of(S)

            def part(j, total):
                n0 = aligned((j // 2) * w, w)
                return total + dot3(pg[j, at], vc[j % 2, n0, :])

            gm[...] = lax.fori_loop(0, p.nm, part, jnp.zeros((size[S], p.nb2), F32))
            for d in range(1, cols):
                gram_sum(d).start()

        @pl.when(t == p.gram_tick + p.lag)
        def _():
            total = gm[...]
            for d in range(1, cols):
                gram_sum(d).wait_recv()
                total = total + gr[d]
            gf[rows_of(S)] = total
            for d in range(1, rows):
                gram_all(d).start()

        @pl.when(t == p.gram_tick + 2 * p.lag)
        def _():
            for d in range(1, rows):
                gram_wait(d).wait_recv()
            nb = p.nb
            one, two = f1[...], f2[...]
            cross = cf[...]
            g11, g21, g22 = gf[:nb, :nb], gf[nb:, :nb], gf[nb:, nb:]
            x1 = exact(exact(one, g11, TN), one)
            key = exact(one, g21, ((0,), (1,))) - 0.5 * exact(x1, cross, TN)
            twist = exact(cross, key, TN)
            gram2 = g22 + twist - twist.T
            x2 = exact(exact(two, gram2, TN), two)
            mixed = exact(key + 0.5 * exact(x1, cross), two)
            skw[:nb, :nb] = 0.5 * (x1.T - x1)
            skw[:nb, nb:] = mixed
            skw[nb:, :nb] = -mixed.T
            skw[nb:, nb:] = 0.5 * (x2.T - x2)

        j = t - p.done - p.zlag * hops

        @pl.when(jnp.logical_and(jnp.logical_and(j >= 0, j < p.nm), j % 2 == core))
        def _():
            i = j // 2
            for b in range(w // step):
                at = aligned(i * w + b * step, step)
                lp[at] = -dot3(pr[i, :, pl.ds(b * step, step)].T, comp[...])

        @pl.when(t + 1 < p.nch)
        def _():
            fetch(t + 1)

        @pl.when(t < p.nch)
        def _():
            slot = t % 2
            pltpu.make_async_copy(mbuf.at[slot], mbuf.at[slot], m_in.at[slot]).wait()
            high, low = split(mbuf[slot])
            both = dot(vt[...], high)
            pt[t] = both[: p.nb2] + both[p.nb2 :] + dot(vt[pl.ds(0, p.nb2)], low)
            rs(t, 0).start()

        jn = t + 1 - p.done

        @pl.when(jnp.logical_and(jn >= 0, jn < p.nm))
        def _():
            @pl.when(jn >= 3)
            def _():
                pltpu.make_async_copy(
                    tbuf.at[jn % 3], t_hbm.at[:, pl.ds(column(jn), w)], t_out.at[jn % 3]
                ).wait()

            m_copy(jn, tbuf, jn % 3, t_in.at[jn % 3]).start()

        @pl.when(t == p.done - 1)
        def _():
            for d in range(1, rows):
                cross_got(d).wait_recv()
            nb = p.nb
            comp[:nb, :nb] = f1[...]
            comp[:nb, nb:] = -exact(exact(f1[...], cf[...]), f2[...])
            comp[nb:, :nb] = jnp.zeros((nb, nb), F32)
            comp[nb:, nb:] = f2[...]

            def build(i, _):
                at = aligned(i * step, step)
                high, low = split(dot3(vown[at, :], comp[...], NT))
                lq[0, at] = high
                lq[1, at] = low
                return 0

            lax.fori_loop(0, nblk, build, 0)

        j = t - p.done

        @pl.when(jnp.logical_and(j >= 0, j < p.nm))
        def _():
            slot = j % 3
            m_copy(j, tbuf, slot, t_in.at[slot]).wait()
            high, low = split(pg[j])

            def add(i, _):
                at = aligned(i * step, step)
                lh = lq[0, at]
                tbuf[slot, at] = tbuf[slot, at] - (dot(lh, high) + dot(lq[1, at], high) + dot(lh, low))
                return 0

            lax.fori_loop(0, nblk, add, 0)
            pltpu.make_async_copy(tbuf.at[slot], t_hbm.at[:, pl.ds(column(j), w)], t_out.at[slot]).start()

        @pl.when(jnp.logical_and(j >= p.nm, j < p.nch))
        def _():
            yb[j - p.nm] = dot3(comp[...], pg[j])

        return 0

    lax.fori_loop(0, p.ticks, tick, 0)

    def left(i, _):
        at = aligned(i * step, step)
        lp[at] = lp[at] + dot3(vown[at, :], skw[...])
        return 0

    lax.fori_loop(0, nblk, left, 0)
    lp_out = pltpu.make_async_copy(lp, lp_hbm, io.at[0])
    lp_out.start()
    outs = []
    for b in range(p.nv):
        copy = pltpu.make_async_copy(yb.at[b], y_hbm.at[:, pl.ds(b * w, w)], io.at[4 + b])
        copy.start()
        outs.append(copy)

    def drain(j, _):
        for s in range(S):
            rs(j, s).wait_send()
            ag(j, s).wait_send()
        return 0

    lax.fori_loop(0, p.nch, drain, 0)

    def drain_z(i, _):
        for s in range(p.nsub):
            @pl.when(jnp.logical_and(c >= q, c < cols - 1))
            def _():
                zcopy(pr.at[i], i, s, zu_s, c + 1).wait_send()

            @pl.when(jnp.logical_and(c <= q, c > 0))
            def _():
                zcopy(pr.at[i], i, s, zd_s, c - 1).wait_send()
        return 0

    lax.fori_loop(0, p.nz, drain_z, 0)

    def drain_v(i, _):
        @pl.when(pos < cols - 1)
        def _():
            ring(i, 0, va_s, va_r, nxt).wait_send()

        @pl.when(posb < cols - 1)
        def _():
            ring(i, half, vb_s, vb_r, prv).wait_send()

        cross_core(core, i, 0, 0).wait_send()
        cross_core(core, i, half, 1).wait_send()
        return 0

    lax.fori_loop(0, p.np, drain_v, 0)
    for d in range(1, rows):
        cross_sum(d).wait_send()
        cross_all(d).wait_send()
        gram_all(d).wait_send()
    for d in range(1, cols):
        gram_sum(d).wait_send()
    for j in range(max(0, p.nm - 3), p.nm):
        pltpu.make_async_copy(tbuf.at[j % 3], t_hbm.at[:, pl.ds(column(j), w)], t_out.at[j % 3]).wait()
    pltpu.make_async_copy(vc, vc_hbm, io.at[3]).wait()
    vj_out.wait()
    lp_out.wait()
    for copy in outs:
        copy.wait()


def exchange(p, matrix, vectors, first, second, factor1, factor2):
    n, nb2, w, S = p.n, p.nb2, p.w, p.stages
    hbm = pl.BlockSpec(memory_space=pl.ANY)
    vmem = pl.BlockSpec(memory_space=pltpu.VMEM)
    dma = pltpu.SemaphoreType.DMA

    def body(*refs):
        ins, rest = refs[:11], refs[11:]
        before, rest = rest[:7], rest[7:]
        recvs, rest = rest[:S], rest[S:]
        kernel(p, *ins, *before, recvs, *rest)

    shape = lambda *s: jax.ShapeDtypeStruct(s, F32)
    scratch = [
        pltpu.VMEM((n, nb2), F32),
        pltpu.VMEM((2 * nb2, n), BF16),
        pltpu.VMEM((2, n, nb2), BF16),
        pltpu.VMEM((2, n, w), F32),
        pltpu.VMEM((3, n, w), F32),
        pltpu.VMEM((p.nch, nb2, w), F32),
        pltpu.VMEM((p.nch, nb2, w), F32),
    ]
    scratch += [pltpu.VMEM((p.nch, nb2 >> (s + 1), w), F32) for s in range(S)]
    scratch += [
        pltpu.VMEM((p.nz, nb2, w), F32),
        pltpu.VMEM((2, n, nb2), F32),
        pltpu.VMEM((n, nb2), F32),
        pltpu.VMEM((p.nv, nb2, w), F32),
        pltpu.VMEM((p.nb, p.nb), F32),
        pltpu.VMEM((p.rows, p.piece, p.nb), F32),
        pltpu.VMEM((p.nb, p.nb), F32),
        pltpu.VMEM((nb2 >> S, nb2), F32),
        pltpu.VMEM((p.cols, nb2 >> S, nb2), F32),
        pltpu.VMEM((nb2, nb2), F32),
        pltpu.VMEM((nb2, nb2), F32),
        pltpu.VMEM((nb2, nb2), F32),
    ]
    scratch += [dma((p.nch, S)) for _ in range(4)]
    scratch += [dma((p.nz, p.nsub)) for _ in range(3)]
    scratch += [dma((p.np,)) for _ in range(4)] + [dma((2, p.np)) for _ in range(2)]
    scratch += [dma((p.rows,)) for _ in range(4)]
    scratch += [dma((p.cols,)) for _ in range(2)] + [dma((p.rows,)) for _ in range(2)]
    scratch += [dma((2,)), dma((3,)), dma((3,)), dma((4 + p.nv,))]
    return pl.pallas_call(
        body,
        out_shape=[shape(n, p.nc), shape(n, nb2), shape(2, n, nb2), shape(nb2, p.kc), shape(n, nb2)],
        in_specs=[hbm] * 4 + [vmem] * 2,
        out_specs=[hbm] * 5,
        scratch_shapes=scratch,
        compiler_params=pltpu.CompilerParams(
            collective_id=0, has_side_effects=True, vmem_limit_bytes=VMEM_BYTES
        ),
        cost_estimate=pl.CostEstimate(
            flops=12 * n * p.nc * nb2, bytes_accessed=12 * n * p.nc, transcendentals=0
        ),
    )(matrix, vectors, first, second, factor1, factor2)


def finish_step(nm, lp_ref, vj_ref, vc_ref, y_ref, t_ref, vec_ref, out_ref, back_ref, left, own):
    step = pl.program_id(0)
    n, nb2 = lp_ref.shape

    @pl.when(step == 0)
    def _():
        def prepare(i, _):
            at = aligned(i * 256, 256)
            for src, dst in ((lp_ref, left), (vj_ref, own)):
                high, low = split(src[at, :])
                dst[at, pl.ds(0, nb2)] = high
                dst[at, pl.ds(nb2, nb2)] = low
                dst[at, pl.ds(2 * nb2, nb2)] = high
            return 0

        lax.fori_loop(0, n // 256, prepare, 0)

    @pl.when(step < nm)
    def _():
        high, low = split(vc_ref[...])
        right = jnp.concatenate([high, high, low], axis=1)
        out_ref[...] = t_ref[...] - dot(left[...], right, NT)

    @pl.when(step >= nm)
    def _():
        high, low = split(y_ref[...])
        right = jnp.concatenate([high, high, low], axis=0)
        back_ref[...] = vec_ref[...] - dot(own[...], right)


def finish(p, partly, left, panel, inner, joined, vectors):
    n, nb2, w = p.n, p.nb2, min(512, p.kc)
    nm, nv = p.nc // w, p.kc // w
    one = lambda i: jnp.minimum(i, nm - 1)
    two = lambda i: jnp.maximum(i - nm, 0)
    whole = pl.BlockSpec((n, nb2), lambda i: (0, 0))
    matrix_block = pl.BlockSpec((n, w), lambda i: (0, one(i)))
    vector_block = pl.BlockSpec((n, w), lambda i: (0, two(i)))
    return pl.pallas_call(
        functools.partial(finish_step, nm),
        grid=(nm + nv,),
        out_shape=[jax.ShapeDtypeStruct((n, p.nc), F32), jax.ShapeDtypeStruct((n, p.kc), F32)],
        in_specs=[
            whole,
            whole,
            pl.BlockSpec((w, nb2), lambda i: (one(i), 0)),
            pl.BlockSpec((nb2, w), lambda i: (0, two(i))),
            matrix_block,
            vector_block,
        ],
        out_specs=[matrix_block, vector_block],
        scratch_shapes=[pltpu.VMEM((n, 3 * nb2), BF16), pltpu.VMEM((n, 3 * nb2), BF16)],
        compiler_params=pltpu.CompilerParams(vmem_limit_bytes=VMEM_BYTES),
    )(left, joined, panel, inner, partly, vectors)


def solution(mesh):
    rows, cols = mesh.shape["row"], mesh.shape["col"]

    def shards(matrix, first, factor1, second, factor2, vectors):
        p = Plan(rows, cols, *matrix.shape, vectors.shape[1], first.shape[1])
        partly, left, panel, inner, joined = exchange(p, matrix, vectors, first, second, factor1, factor2)
        panel = panel.reshape(2 * p.n, 2 * p.nb)
        return tuple(finish(p, partly, left, panel, inner, joined, vectors))

    in_specs = (P("row", "col"), P("row", None), P(), P("row", None), P(), P("row", "col"))
    out_specs = (P("row", "col"), P("row", "col"))
    return jax.shard_map(shards, mesh=mesh, in_specs=in_specs, out_specs=out_specs, check_vma=False)
```
